32 devices in a mesh: groups: 2 (over y), row: 4 (over z), col: 4 (over x, core).
Axes of the slice: x: 2, y: 2, z: 4, core: 2. Of those that a mesh axis runs over, the one named last changes fastest.
Arguments:
- prev_solution: float32 [16384, 1024], P(None, ('groups', 'row', 'col')), parts along dimension 1, may hold values from -6 to 6
- factor_panel: float32 [1024, 16384], P(None, ('row', 'col')), may hold values from -0.0625 to 0.0625
- right_side: float32 [1024, 1024], P('row', ('groups', 'col')), parts along dimension 1, may hold values from -6 to 6
- window_factor: float32 [1024, 1024], P('row'), may hold values from -2 to 2, as said below
Outputs:
- window_solution: float32 [1024, 1024], P('row', ('groups', 'col')), parts along dimension 1
The draws below stay inside these ranges and needn't reach their ends.
There are 2 independent parts, one for each index of `groups`. The reference program is written for one: setup_inputs(seed, part) draws one part's arguments, and reference() takes and returns one part's arrays. A program takes and returns all parts, laid end to end along the dimension named above; an argument that names none is the same for every part. Nothing has to cross between parts.
Inputs may be any that keep to these rules, and one draw needn't show every extreme that they name: `window_factor`: lower triangular, with diagonal entries between 1 and 2.
All inputs are finite; a program needn't handle non-finite values.
Results may differ from the reference program's by a relative error of at most 0.0003.
Values sent between devices are 32-bit elements; how exact they have to be, the bound alone decides.
No kernel may reach another device: no remote copies, remote signals or barrier semaphores. Data moves between devices by JAX's collectives and lax.ppermute only.
A program may use at most 64 MiB of HBM per device.

```python
import math
import jax
import jax.numpy as jnp
from jax import lax

W = 1024
Q = 512
PREV = 16384


def draw_window_factor(key, part):
    key_lower, key_diag, key_rate = jax.random.split(key, 3)
    row_index = jnp.arange(W)[:, None]
    col_index = jnp.arange(W)[None, :]
    lower_part = jnp.clip(jax.random.normal(key_lower, (W, W), jnp.float32), -4.0, 4.0)
    log_gap = jax.random.uniform(key_rate, (W,), jnp.float32, math.log(0.01), math.log(0.2))
    lower_part = lower_part * (0.12 / math.sqrt(W))
    diag_values = jax.random.uniform(key_diag, (W,), jnp.float32, 1.0, 2.0)
    carry_rate = 1.0 - jnp.exp(log_gap)
    sub_values = -carry_rate * diag_values
    diag_full = jnp.broadcast_to(diag_values[:, None], (W, W))
    sub_full = jnp.broadcast_to(sub_values[:, None], (W, W))
    below = jnp.where(row_index == col_index + 1, sub_full + lower_part, lower_part)
    return jnp.where(row_index > col_index, below, jnp.where(row_index == col_index, diag_full, 0.0))


def spiked(array, own_key, source, target, blocks, factor):
    owner, partner = [(jnp.arange(array.shape[dim]) // (array.shape[dim] // blocks)).reshape([-1 if axis == dim else 1 for axis in range(array.ndim)]) for dim in (source, target)]
    chosen = jax.random.permutation(own_key, blocks)[partner]
    strong = (owner == chosen) | (owner == (partner + blocks // 2) % blocks)
    return jnp.where(strong, factor * array, array)


def level_of(stream_key, extent, pieces, smallest, largest):
    factor_of, own = 1.0, jax.random.fold_in(stream_key, 6)
    for dim, blocks in pieces:
        steps = jnp.exp(jax.random.uniform(jax.random.fold_in(own, dim), (blocks,), jnp.float32, smallest / len(pieces), largest / len(pieces)))
        factor_of = factor_of * jnp.repeat(steps, extent[dim] // blocks).reshape([-1 if axis == dim else 1 for axis in range(len(extent))])
    return factor_of


def noise(own_key, shape, deviation, bound, cuts=(), kind=jnp.bfloat16):
    result = deviation * jax.random.normal(own_key, shape, jnp.float32)
    if cuts:
        result = result * level_of(own_key, shape, cuts, -0.22, 0.18)
    return jnp.clip(result, -bound, bound).astype(kind)


def noise_with(stream_key, shape, width, most, cuts, heavy, held_as=jnp.bfloat16):
    values = width * jax.random.normal(stream_key, shape, jnp.float32)
    if cuts:
        values = values * level_of(stream_key, shape, cuts, -0.22, 0.18)
    return jnp.clip(spiked(values, jax.random.fold_in(stream_key, 3), *heavy), -most, most).astype(held_as)


def setup_inputs(seed: int = 0, part: int = 0) -> dict:
    keys = jax.random.split(jax.random.key(seed), 5)
    part_keys = jax.random.split(jax.random.fold_in(keys[4], part), 5)
    prev_solution = noise(part_keys[0], (PREV, Q), 1.0, 6.0, ((1, 16),), jnp.float32)
    factor_panel = noise_with(keys[1], (W, PREV), PREV ** -0.5, 0.0625, ((1, 16),), (1, 0, 16, 2.0), jnp.float32)
    right_side = noise(part_keys[2], (W, Q), 1.0, 6.0, ((0, 4), (1, 4)), jnp.float32)
    window_factor = draw_window_factor(jax.random.fold_in(keys[4], 71), part)
    return {"prev_solution": prev_solution, "factor_panel": factor_panel, "right_side": right_side, "window_factor": window_factor}


def reference(prev_solution, factor_panel, right_side, window_factor):
    coupling = jnp.dot(factor_panel.astype(jnp.float32), prev_solution.astype(jnp.float32), precision=lax.Precision.HIGHEST, preferred_element_type=jnp.float32)
    residual = right_side - coupling
    return jax.scipy.linalg.solve_triangular(window_factor, residual, lower=True)
```

```python
import functools

import jax
import jax.numpy as jnp
from jax import lax
from jax.experimental import pallas as pl
from jax.experimental.pallas import tpu as pltpu
from jax.sharding import PartitionSpec as P

HIGHEST = lax.Precision.HIGHEST


def dot_exact(a, b):
    return jnp.dot(a, b, precision=HIGHEST, preferred_element_type=jnp.float32)


def invert_kernel(block_ref, inverse_ref):
    count, size, _ = block_ref.shape
    rows = lax.broadcasted_iota(jnp.int32, (size, size), 0)
    cols = lax.broadcasted_iota(jnp.int32, (size, size), 1)
    blocks = [block_ref[t] for t in range(count)]
    inverses = []
    for block in blocks:
        diagonal = jnp.sum(jnp.where(rows == cols, block, 0.0), axis=1, keepdims=True)
        inverses.append(jnp.where(rows == cols, 1.0 / diagonal, 0.0))
    step = 1
    while step < size:
        below = ((rows // step) % 2 == 1) & (cols // step == rows // step - 1)
        for t in range(count):
            coupled = dot_exact(jnp.where(below, blocks[t], 0.0), inverses[t])
            inverses[t] = inverses[t] - dot_exact(inverses[t], coupled)
        step *= 2
    for t in range(count):
        inverse_ref[t] = inverses[t]


def invert_blocks(blocks):
    return pl.pallas_call(
        invert_kernel,
        out_shape=jax.ShapeDtypeStruct(blocks.shape, jnp.float32),
        in_specs=[pl.BlockSpec(memory_space=pltpu.VMEM)],
        out_specs=pl.BlockSpec(memory_space=pltpu.VMEM),
        cost_estimate=pl.CostEstimate(flops=6 * 10**8, bytes_accessed=10**6, transcendentals=0),
    )(blocks)


def solve_kernel(size, factor_ref, right_ref, kept_ref, arrived_ref, solved_ref):
    rows = right_ref.shape[0]
    for start in range(0, rows, size):
        here = pl.ds(start, size)
        residual = right_ref[here, :] - (kept_ref[here, :] + arrived_ref[here, :])
        if start:
            residual = residual - dot_exact(factor_ref[here, pl.ds(0, start)], solved_ref[pl.ds(0, start), :])
        solved_ref[here, :] = dot_exact(factor_ref[here, here], residual)


def solve_window(size, factor, right, kept, arrived):
    return pl.pallas_call(
        functools.partial(solve_kernel, size),
        out_shape=jax.ShapeDtypeStruct(right.shape, jnp.float32),
        in_specs=[pl.BlockSpec(memory_space=pltpu.VMEM)] * 4,
        out_specs=pl.BlockSpec(memory_space=pltpu.VMEM),
        cost_estimate=pl.CostEstimate(flops=2 * 10**9, bytes_accessed=6 * 10**6, transcendentals=0),
    )(factor, right, kept, arrived)


def swap(value, axis, step):
    return lax.ppermute(value, axis, [(i, i ^ step) for i in range(lax.axis_size(axis))])


def place(mine, theirs, bit, dim):
    first = jnp.where(bit == 0, mine, theirs)
    second = jnp.where(bit == 0, theirs, mine)
    return jnp.stack([first, second], axis=dim)


def gather_window(strip, row_index, group_index, col_index):
    row_count, col_count, group_count = (lax.axis_size(a) for a in ("row", "col", "groups"))
    strip_rows, window = strip.shape
    if row_count != 4 or col_count != 4 or group_count != 2:
        return lax.all_gather(strip, "row", axis=0, tiled=True)
    share_rows = strip_rows // (group_count * col_count)
    share = lax.dynamic_slice_in_dim(strip, (group_index * col_count + col_index) * share_rows, share_rows, 0)
    shares = jnp.zeros((row_count, share_rows, window), jnp.float32)
    shares = lax.dynamic_update_slice_in_dim(shares, share[None], row_index, 0)
    for step in (3, 2, 1):
        shares = lax.dynamic_update_slice_in_dim(shares, swap(share, "row", step)[None], row_index ^ step, 0)
    shares = place(shares, swap(shares, "col", 2), col_index >> 1, 1)
    shares = place(shares, swap(shares, "groups", 1), group_index, 1)
    shares = place(shares, swap(shares, "col", 1), col_index & 1, 3)
    return shares.reshape(row_count * strip_rows, window)


def shards(prev_solution, factor_panel, right_side, window_factor):
    row_count, col_count = lax.axis_size("row"), lax.axis_size("col")
    row_index, col_index, group_index = (lax.axis_index(a) for a in ("row", "col", "groups"))
    strip_rows, strip_cols = right_side.shape
    window = window_factor.shape[1]
    size = min(128, strip_rows)

    by_rows = lax.all_to_all(prev_solution, ("row", "col"), split_axis=0, concat_axis=1, tiled=True)

    own = lax.dynamic_slice_in_dim(window_factor, row_index * strip_rows, strip_rows, 1)
    blocks = jnp.stack([own[t : t + size, t : t + size] for t in range(0, strip_rows, size)])
    inverses = invert_blocks(blocks)
    strip = window_factor
    for t in range(strip_rows // size):
        strip = lax.dynamic_update_slice(strip, inverses[t], (t * size, row_index * strip_rows + t * size))
    factor = gather_window(strip, row_index, group_index, col_index)
    right = lax.dynamic_update_slice_in_dim(
        jnp.zeros((window, strip_cols), jnp.float32), right_side, row_index * strip_rows, 0
    )

    partial = jnp.dot(factor_panel, by_rows, precision=lax.Precision.HIGH, preferred_element_type=jnp.float32)

    def block(index):
        return lax.dynamic_slice_in_dim(partial, index * strip_cols, strip_cols, 1)

    if col_count == 4:
        sent = jnp.concatenate([block(col_index ^ 3), block(col_index ^ 1)], axis=0)
        landed = swap(sent, "col", 1)
        far = block(col_index ^ 2) + landed[:window]
        kept = block(col_index) + landed[window:]
        arrived = swap(far, "col", 2)
    else:
        kept = lax.psum_scatter(partial, "col", scatter_dimension=1, tiled=True)
        arrived = jnp.zeros_like(kept)

    solved = solve_window(size, factor, right, kept, arrived)

    if row_count == 4:
        total = lax.dynamic_slice_in_dim(solved, row_index * strip_rows, strip_rows, 0)
        for step in (3, 2, 1):
            part = lax.dynamic_slice_in_dim(solved, (row_index ^ step) * strip_rows, strip_rows, 0)
            total = total + swap(part, "row", step)
        return total
    return lax.psum_scatter(solved, "row", scatter_dimension=0, tiled=True)


def solution(mesh):
    in_specs = (
        P(None, ("groups", "row", "col")),
        P(None, ("row", "col")),
        P("row", ("groups", "col")),
        P("row", None),
    )
    out_specs = P("row", ("groups", "col"))
    return jax.shard_map(shards, mesh=mesh, in_specs=in_specs, out_specs=out_specs, check_vma=False)
```

```python
import functools
import math

import jax
import jax.numpy as jnp
from jax import lax
from jax.experimental import pallas as pl
from jax.experimental.pallas import tpu as pltpu
from jax.sharding import Mesh
from jax.sharding import PartitionSpec as P

HIGHEST = lax.Precision.HIGHEST
SIZE = 128
VMEM = pl.BlockSpec(memory_space=pltpu.VMEM)
SMEM = pl.BlockSpec(memory_space=pltpu.SMEM)
QUERY_CUTS = (32,)


def exact(a, b):
    return jnp.dot(a, b, precision=HIGHEST, preferred_element_type=jnp.float32)


def exact_t(a, b):
    return lax.dot_general(a, b, (((1,), (1,)), ((), ())), precision=HIGHEST, preferred_element_type=jnp.float32)


def call(kernel, outs, scratch=(), flops=10**6, scalars=0, spare=4):
    def run(*args):
        moved = sum(a.size * a.dtype.itemsize for a in args)
        held = sum(math.prod(a.shape) * a.dtype.itemsize for a in (*jax.tree.leaves(outs), *scratch))
        return pl.pallas_call(
            kernel,
            out_shape=outs,
            in_specs=[SMEM] * scalars + [VMEM] * (len(args) - scalars),
            out_specs=jax.tree.map(lambda _: VMEM, outs),
            scratch_shapes=list(scratch),
            cost_estimate=pl.CostEstimate(flops=flops, bytes_accessed=moved, transcendentals=0),
            compiler_params=pltpu.CompilerParams(vmem_limit_bytes=moved + held + spare * 2**20),
        )(*args)

    return run


def shape(*dims, dtype=jnp.float32):
    return jax.ShapeDtypeStruct(dims, dtype)


def prepare_kernel(factor_ref, ready_ref):
    rows = lax.broadcasted_iota(jnp.int32, (SIZE, SIZE), 0)
    cols = lax.broadcasted_iota(jnp.int32, (SIZE, SIZE), 1)
    starts = range(0, factor_ref.shape[0], SIZE)
    blocks = [factor_ref[pl.ds(s, SIZE), pl.ds(s, SIZE)] for s in starts]
    inverses = []
    for block in blocks:
        diagonal = jnp.sum(jnp.where(rows == cols, block, 0.0), axis=1, keepdims=True)
        inverses.append(jnp.where(rows == cols, 1.0 / diagonal, 0.0))
    step = 1
    while step < SIZE:
        below = ((rows // step) % 2 == 1) & (cols // step == rows // step - 1)
        coupled = [exact(jnp.where(below, b, 0.0), i) for b, i in zip(blocks, inverses)]
        inverses = [i - exact(i, c) for i, c in zip(inverses, coupled)]
        step *= 2
    for start, inverse in zip(starts, inverses):
        if start:
            ready_ref[pl.ds(start, SIZE), pl.ds(0, start)] = exact(
                inverse, factor_ref[pl.ds(start, SIZE), pl.ds(0, start)]
            )
        ready_ref[pl.ds(start, SIZE), pl.ds(start, SIZE)] = inverse


def halves(value):
    high = value.astype(jnp.bfloat16)
    return high, (value - high.astype(jnp.float32)).astype(jnp.bfloat16)


def split_kernel(ref, high_ref, low_ref):
    for start in range(0, ref.shape[0], 128):
        here = pl.ds(start, 128)
        high_ref[here, :], low_ref[here, :] = halves(ref[here, :])


def split(value, flops):
    return call(split_kernel, [shape(*value.shape, dtype=jnp.bfloat16)] * 2, flops=flops)(value)


def couple_kernel(side_ref, core_ref, queries_ref, *refs):
    *factor_refs, kept_ref, far_ref, q_high, q_low = refs
    count = kept_ref.shape[0]
    columns = factor_refs[0].shape[1]
    for part in range(2):
        rows = pl.ds(pl.multiple_of(((side_ref[0] + part) % 2) * count, 8), count)
        for half in range(2):
            cols = pl.ds(pl.multiple_of(((core_ref[0] + half) % 2) * columns, 128), columns)
            here = (pl.ds(part * count, count), pl.ds(half * columns, columns))
            q_high[here], q_low[here] = halves(queries_ref[rows, cols])

    def product(a, b):
        return lax.dot_general(a, b, (((1,), (1,)), ((), ())), preferred_element_type=jnp.float32)

    for start in range(0, kept_ref.shape[1], 256):
        here = pl.ds(start, 256)
        total = 0.0
        for half in range(2):
            cols = pl.ds(half * columns, columns)
            high, low = (ref[here, :] for ref in factor_refs[2 * half : 2 * half + 2])
            total = total + product(q_high[:, cols], high)
            total = total + product(q_low[:, cols], high) + product(q_high[:, cols], low)
        kept_ref[:, here] = total[:count]
        far_ref[:, here] = total[count:]


def solve_kernel(row_ref, ready_ref, right_ref, kept_ref, arrived_ref, *out_refs):
    *piece_refs, left = out_refs
    strip = right_ref.shape[1]
    window = kept_ref.shape[1]
    row = row_ref[0]
    left[...] = -(kept_ref[...] + arrived_ref[...])
    own = pl.ds(pl.multiple_of(row * strip, strip), strip)
    left[:, own] = left[:, own] + right_ref[...]
    blocks = []
    for start in range(0, window, SIZE):
        here = pl.ds(start, SIZE)
        blocks.append(exact_t(left[:, here], ready_ref[here, here]))
    for i, start in enumerate(range(0, window, SIZE)):
        left[:, pl.ds(start, SIZE)] = blocks[i]
        for k in range(i + 1, len(blocks)):
            blocks[k] = blocks[k] - exact_t(blocks[i], ready_ref[pl.ds(k * SIZE, SIZE), pl.ds(start, SIZE)])
    for step, piece_ref in enumerate(piece_refs):
        piece_ref[...] = left[:, pl.ds(pl.multiple_of((row ^ step) * strip, strip), strip)]


def sum_kernel(core_ref, *refs):
    *piece_refs, own_ref, other_ref, total = refs
    value = piece_refs[0][...]
    for ref in piece_refs[1:]:
        value = value + ref[...]
    total[...] = value
    count = own_ref.shape[0]
    own_ref[...] = total[pl.ds(pl.multiple_of(core_ref[0] * count, 8), count), :]
    other_ref[...] = total[pl.ds(pl.multiple_of((1 - core_ref[0]) * count, 8), count), :]


def finish_kernel(cuts, core_ref, *refs):
    *part_refs, out_ref, total = refs
    offset = 0
    width = sum(cuts)
    for cut, own_ref, other_ref in zip(cuts, part_refs[::2], part_refs[1::2]):
        for ref, core in ((own_ref, core_ref[0]), (other_ref, 1 - core_ref[0])):
            for side in range(2):
                place = pl.multiple_of(side * 2 * width + core * width + offset, 8)
                total[pl.ds(place, cut), :] = ref[pl.ds(side * cut, cut), :]
        offset += cut
    out_ref[...] = total[...].T


def swap(value, axis, step):
    return lax.ppermute(value, axis, [(i, i ^ step) for i in range(lax.axis_size(axis))])


def place(mine, theirs, bit, dim):
    first = jnp.where(bit == 0, mine, theirs)
    second = jnp.where(bit == 0, theirs, mine)
    return jnp.stack([first, second], axis=dim)


def gather_window(strip, row, group, side, core, first, second):
    strip_rows, window = strip.shape
    share_rows = strip_rows // 8
    share = lax.dynamic_slice_in_dim(strip, (group * 4 + side * 2 + core) * share_rows, share_rows, 0)
    landed = [swap(share, "row", step) for step in (3, 2, 1)]
    landed, first = lax.optimization_barrier((landed, first()))
    shares = jnp.zeros((4, share_rows, window), jnp.float32)
    shares = lax.dynamic_update_slice_in_dim(shares, share[None], row, 0)
    for step, value in zip((3, 2, 1), landed):
        shares = lax.dynamic_update_slice_in_dim(shares, value[None], row ^ step, 0)
    near, far = shares[:, :, : window // 2], shares[:, :, window // 2 :]
    near_other, far_other = swap(near, "side", 1), swap(far, "groups", 1)
    near, far = place(near, near_other, side, 1), place(far, far_other, group, 1)
    near_other, far_other = swap(near, "groups", 1), swap(far, "side", 1)
    (near_other, far_other), second = lax.optimization_barrier(((near_other, far_other), second()))
    near, far = place(near, near_other, group, 1), place(far, far_other, side, 2)
    return jnp.concatenate([near, far], axis=-1), first, second


def shards(prev_solution, factor_panel, right_side, window_factor):
    row, group, side, core = (lax.axis_index(a) for a in ("row", "groups", "side", "core"))
    row_1, side_1, core_1 = (jnp.full((1,), v, jnp.int32) for v in (row, side, core))
    strip_rows, strip_cols = right_side.shape
    window = window_factor.shape[1]

    shares, own, other = gather_window(
        window_factor,
        row,
        group,
        side,
        core,
        lambda: split(factor_panel, 5 * 10**10),
        lambda: split(swap(factor_panel, "core", 1), 10**6),
    )
    width = prev_solution.shape[1]
    right = right_side.T.reshape(2, 2, width, strip_rows)
    right_own = lax.dynamic_index_in_dim(right, core, 1, keepdims=False)
    right_other = swap(lax.dynamic_index_in_dim(right, 1 - core, 1, keepdims=False), "core", 1)
    right = place(right_own, right_other, core, 0)

    offset = 0
    parts = []
    for cut in QUERY_CUTS:
        stream = prev_solution[:, offset : offset + cut]
        queries = lax.all_to_all(stream, ("row", "side"), split_axis=0, concat_axis=1, tiled=True).T
        half = queries.shape[0] // 2
        if not offset:
            queries, shares = lax.optimization_barrier((queries, shares))
            factor = place(shares, swap(shares, "core", 1), core, 3).reshape(window, window)
            ready = call(prepare_kernel, shape(window, window))(factor)
        kept, far = call(
            couple_kernel,
            [shape(half, window)] * 2,
            [pltpu.VMEM(queries.shape, jnp.bfloat16)] * 2,
            scalars=2,
        )(side_1, core_1, queries, *own, *other)
        pieces = call(
            solve_kernel, [shape(half, strip_rows)] * 4, [pltpu.VMEM((half, window), jnp.float32)], scalars=1
        )(row_1, ready, right[:, :, offset : offset + cut].reshape(half, strip_rows), kept, swap(far, "side", 1))
        landed = [swap(pieces[step], "row", step) for step in (3, 2, 1)]
        own, other = call(
            sum_kernel, [shape(half // 2, strip_rows)] * 2, [pltpu.VMEM((half, strip_rows), jnp.float32)], scalars=1
        )(core_1, pieces[0], *landed)
        parts += [own, swap(other, "core", 1)]
        offset += cut
    return call(
        functools.partial(finish_kernel, QUERY_CUTS),
        shape(strip_rows, strip_cols),
        [pltpu.VMEM((strip_cols, strip_rows), jnp.float32)],
        scalars=1,
    )(core_1, *parts)


def shards_any(prev_solution, factor_panel, right_side, window_factor):
    row = lax.axis_index("row")
    strip_rows, strip_cols = right_side.shape
    by_rows = lax.all_to_all(prev_solution, ("row", "col"), split_axis=0, concat_axis=1, tiled=True)
    factor = lax.all_gather(window_factor, "row", axis=0, tiled=True)
    right = jnp.zeros((factor.shape[0], strip_cols), jnp.float32)
    right = lax.dynamic_update_slice_in_dim(right, right_side, row * strip_rows, 0)
    partial = exact(factor_panel, by_rows)
    coupling = lax.psum_scatter(partial, "col", scatter_dimension=1, tiled=True)
    solved = jax.scipy.linalg.solve_triangular(factor, right - coupling, lower=True)
    return lax.psum_scatter(solved, "row", scatter_dimension=0, tiled=True)


def solution(mesh):
    staged = mesh.shape["groups"] == 2 and mesh.shape["row"] == 4 and mesh.shape["col"] == 4
    if staged:
        mesh = Mesh(mesh.devices.reshape(2, 4, 2, 2), ("groups", "row", "side", "core"))
    col = ("side", "core") if staged else ("col",)
    in_specs = (P(None, ("groups", "row", *col)), P(None, ("row", *col)), P("row", ("groups", *col)), P("row", None))
    out_specs = P("row", ("groups", *col))
    body = shards if staged else shards_any
    return jax.shard_map(body, mesh=mesh, in_specs=in_specs, out_specs=out_specs, check_vma=False)
```

```python
import functools
import math

import jax
import jax.numpy as jnp
from jax import lax
from jax.experimental import pallas as pl
from jax.experimental.pallas import tpu as pltpu
from jax.sharding import Mesh
from jax.sharding import PartitionSpec as P

HIGHEST = lax.Precision.HIGHEST
SIZE = 128
VMEM = pl.BlockSpec(memory_space=pltpu.VMEM)
SMEM = pl.BlockSpec(memory_space=pltpu.SMEM)
QUERY_CUTS = (32,)


def exact(a, b):
    return jnp.dot(a, b, precision=HIGHEST, preferred_element_type=jnp.float32)


def exact_t(a, b):
    return lax.dot_general(a, b, (((1,), (1,)), ((), ())), precision=HIGHEST, preferred_element_type=jnp.float32)


def call(kernel, outs, scratch=(), flops=10**6, scalars=0, spare=4):
    def run(*args):
        moved = sum(a.size * a.dtype.itemsize for a in args)
        held = sum(math.prod(a.shape) * a.dtype.itemsize for a in (*jax.tree.leaves(outs), *scratch))
        return pl.pallas_call(
            kernel,
            out_shape=outs,
            in_specs=[SMEM] * scalars + [VMEM] * (len(args) - scalars),
            out_specs=jax.tree.map(lambda _: VMEM, outs),
            scratch_shapes=list(scratch),
            cost_estimate=pl.CostEstimate(flops=flops, bytes_accessed=moved, transcendentals=0),
            compiler_params=pltpu.CompilerParams(vmem_limit_bytes=moved + held + spare * 2**20),
        )(*args)

    return run


def shape(*dims, dtype=jnp.float32):
    return jax.ShapeDtypeStruct(dims, dtype)


def share_kernel(where_ref, strip_ref, share_ref):
    row, group, side, core = (where_ref[i] for i in range(4))
    count = share_ref.shape[0]
    start = (group * 4 + side * 2 + core) * count
    share_ref[...] = strip_ref[pl.ds(pl.multiple_of(start, 8), count), :]


def rows_kernel(where_ref, share_ref, *refs):
    *landed_refs, near_ref, far_ref = refs
    half = near_ref.shape[2]
    for step, ref in enumerate((share_ref, *landed_refs)):
        near_ref[where_ref[0] ^ step] = ref[:, pl.ds(0, half)]
        far_ref[where_ref[0] ^ step] = ref[:, pl.ds(half, half)]


def first_kernel(where_ref, near_ref, near_other_ref, far_ref, far_other_ref, near_out, far_out):
    row, group, side, core = (where_ref[i] for i in range(4))
    near_out[side] = near_ref[...]
    near_out[1 - side] = near_other_ref[...]
    far_out[group] = far_ref[...]
    far_out[1 - group] = far_other_ref[...]


def second_kernel(where_ref, near_ref, near_other_ref, far_ref, far_other_ref, out_ref):
    row, group, side, core = (where_ref[i] for i in range(4))
    half = near_ref.shape[3]
    for r in range(4):
        for i in range(2):
            out_ref[r, group, i, :, pl.ds(0, half)] = near_ref[i, r]
            out_ref[r, 1 - group, i, :, pl.ds(0, half)] = near_other_ref[i, r]
            out_ref[r, i, side, :, pl.ds(half, half)] = far_ref[i, r]
            out_ref[r, i, 1 - side, :, pl.ds(half, half)] = far_other_ref[i, r]


def prepare_kernel(where_ref, own_ref, other_ref, ready_ref, factor_ref):
    core = where_ref[3]
    count = own_ref.shape[3]
    for piece in range(16):
        at = (piece // 4, piece // 2 % 2, piece % 2)
        for ref, index in ((own_ref, core), (other_ref, 1 - core)):
            start = pl.multiple_of((2 * piece + index) * count, 8)
            factor_ref[pl.ds(start, count), :] = ref[at]
    rows = lax.broadcasted_iota(jnp.int32, (SIZE, SIZE), 0)
    cols = lax.broadcasted_iota(jnp.int32, (SIZE, SIZE), 1)
    starts = range(0, factor_ref.shape[0], SIZE)
    blocks = [factor_ref[pl.ds(s, SIZE), pl.ds(s, SIZE)] for s in starts]
    inverses = []
    for block in blocks:
        diagonal = jnp.sum(jnp.where(rows == cols, block, 0.0), axis=1, keepdims=True)
        inverses.append(jnp.where(rows == cols, 1.0 / diagonal, 0.0))
    step = 1
    while step < SIZE:
        below = ((rows // step) % 2 == 1) & (cols // step == rows // step - 1)
        coupled = [exact(jnp.where(below, b, 0.0), i) for b, i in zip(blocks, inverses)]
        inverses = [i - exact(i, c) for i, c in zip(inverses, coupled)]
        step *= 2
    for start, inverse in zip(starts, inverses):
        if start:
            ready_ref[pl.ds(start, SIZE), pl.ds(0, start)] = exact(
                inverse, factor_ref[pl.ds(start, SIZE), pl.ds(0, start)]
            )
        ready_ref[pl.ds(start, SIZE), pl.ds(start, SIZE)] = inverse


def right_kernel(where_ref, right_ref, own_ref, other_ref, by_query):
    core = where_ref[3]
    by_query[...] = right_ref[...].T
    width = own_ref.shape[0] // 2
    for side in range(2):
        for ref, index in ((own_ref, core), (other_ref, 1 - core)):
            start = pl.multiple_of((2 * side + index) * width, 8)
            ref[pl.ds(side * width, width), :] = by_query[pl.ds(start, width), :]


def halves(value):
    high = value.astype(jnp.bfloat16)
    return high, (value - high.astype(jnp.float32)).astype(jnp.bfloat16)


def couple_kernel(where_ref, queries_ref, own_ref, other_ref, kept_ref, far_ref, q_high, q_low):
    side, core = where_ref[2], where_ref[3]
    count, window = kept_ref.shape
    columns = own_ref.shape[1]
    for part in range(2):
        rows = pl.ds(pl.multiple_of(((side + part) % 2) * count, 8), count)
        for half in range(2):
            cols = pl.ds(pl.multiple_of(((core + half) % 2) * columns, 128), columns)
            here = (pl.ds(part * count, count), pl.ds(half * columns, columns))
            q_high[here], q_low[here] = halves(queries_ref[rows, cols])

    def product(a, b):
        return lax.dot_general(a, b, (((1,), (1,)), ((), ())), preferred_element_type=jnp.float32)

    for start in range(0, window, 256):
        here = pl.ds(start, 256)
        total = 0.0
        for half, ref in enumerate((own_ref, other_ref)):
            cols = pl.ds(half * columns, columns)
            high, low = halves(ref[here, :])
            total = total + product(q_high[:, cols], high)
            total = total + product(q_low[:, cols], high) + product(q_high[:, cols], low)
        kept_ref[:, here] = total[:count]
        far_ref[:, here] = total[count:]


def deal_kernel(queries_ref, *out_refs):
    columns = out_refs[0].shape[2]
    offset = 0
    for out_ref in out_refs:
        for chip in range(8):
            out_ref[chip] = queries_ref[pl.ds(offset, out_ref.shape[1]), pl.ds(chip * columns, columns)]
        offset += out_ref.shape[1]


def solve_kernel(where_ref, ready_ref, right_own_ref, right_other_ref, kept_ref, arrived_ref, *out_refs):
    *piece_refs, left = out_refs
    count, strip = right_own_ref.shape
    window = kept_ref.shape[1]
    row, core = where_ref[0], where_ref[3]
    left[...] = -(kept_ref[...] + arrived_ref[...])
    cols = pl.ds(pl.multiple_of(row * strip, strip), strip)
    for ref, index in ((right_own_ref, core), (right_other_ref, 1 - core)):
        here = (pl.ds(pl.multiple_of(index * count, 8), count), cols)
        left[here] = left[here] + ref[...]
    for start in range(0, window, SIZE):
        here = pl.ds(start, SIZE)
        left[:, here] = exact_t(left[:, here], ready_ref[here, here])
    for start in range(0, window, 2 * SIZE):
        first, second = pl.ds(start, SIZE), pl.ds(start + SIZE, SIZE)
        left[:, second] = left[:, second] - exact_t(left[:, first], ready_ref[second, first])
        below = pl.ds(start + 2 * SIZE, window - start - 2 * SIZE)
        if below.size:
            both = pl.ds(start, 2 * SIZE)
            left[:, below] = left[:, below] - exact_t(left[:, both], ready_ref[below, both])
    for step, piece_ref in enumerate(piece_refs):
        piece_ref[...] = left[:, pl.ds(pl.multiple_of((row ^ step) * strip, strip), strip)]


def sum_kernel(where_ref, *refs):
    *piece_refs, own_ref, other_ref, total = refs
    value = piece_refs[0][...]
    for ref in piece_refs[1:]:
        value = value + ref[...]
    total[...] = value
    count = own_ref.shape[0]
    own_ref[...] = total[pl.ds(pl.multiple_of(where_ref[3] * count, 8), count), :]
    other_ref[...] = total[pl.ds(pl.multiple_of((1 - where_ref[3]) * count, 8), count), :]


def finish_kernel(cuts, where_ref, *refs):
    *part_refs, out_ref, total = refs
    offset = 0
    width = sum(cuts)
    for cut, own_ref, other_ref in zip(cuts, part_refs[::2], part_refs[1::2]):
        for ref, core in ((own_ref, where_ref[3]), (other_ref, 1 - where_ref[3])):
            for side in range(2):
                place = pl.multiple_of(side * 2 * width + core * width + offset, 8)
                total[pl.ds(place, cut), :] = ref[pl.ds(side * cut, cut), :]
        offset += cut
    out_ref[...] = total[...].T


def swap(value, axis, step):
    return lax.ppermute(value, axis, [(i, i ^ step) for i in range(lax.axis_size(axis))])


def shards(prev_solution, factor_panel, right_side, window_factor):
    row, group, side, core = (lax.axis_index(a) for a in ("row", "groups", "side", "core"))
    where = jnp.stack([row, group, side, core])
    strip_rows, strip_cols = right_side.shape
    window = window_factor.shape[1]
    width = prev_solution.shape[1]
    share_rows, half_window = strip_rows // 8, window // 2

    share = call(share_kernel, shape(share_rows, window), scalars=1)(where, window_factor)
    landed = [swap(share, "row", step) for step in (1, 2, 3)]
    right_own, right_other = call(
        right_kernel,
        [shape(2 * width, strip_rows)] * 2,
        [pltpu.VMEM((strip_cols, strip_rows), jnp.float32)],
        flops=5 * 10**10,
        scalars=1,
    )(where, right_side)
    panel_other = swap(factor_panel, "core", 1)
    landed, right_own = lax.optimization_barrier((landed, right_own))
    right_other = swap(right_other, "core", 1)
    near, far = call(rows_kernel, [shape(4, share_rows, half_window)] * 2, scalars=1)(where, share, *landed)
    near, far = call(first_kernel, [shape(2, 4, share_rows, half_window)] * 2, scalars=1)(
        where, near, swap(near, "side", 1), far, swap(far, "groups", 1)
    )
    near, panel_other = lax.optimization_barrier((near, panel_other))
    shares = call(second_kernel, shape(4, 2, 2, share_rows, window), scalars=1)(
        where, near, swap(near, "groups", 1), far, swap(far, "side", 1)
    )

    dealt = call(deal_kernel, [shape(8, cut, 2 * factor_panel.shape[1]) for cut in QUERY_CUTS])(prev_solution.T)
    offset = 0
    parts = []
    for number, cut in enumerate(QUERY_CUTS):
        queries = lax.all_to_all(dealt[number], ("row", "side"), split_axis=0, concat_axis=0, tiled=True)
        queries = queries.reshape(8 * cut, -1)
        half = 4 * cut
        if not offset:
            queries, shares, right_other = lax.optimization_barrier((queries, shares, right_other))
            ready = call(
                prepare_kernel, shape(window, window), [pltpu.VMEM((window, window), jnp.float32)], scalars=1
            )(where, shares, swap(shares, "core", 1))
        kept, far = call(
            couple_kernel,
            [shape(half, window)] * 2,
            [pltpu.VMEM(queries.shape, jnp.bfloat16)] * 2,
            scalars=1,
        )(where, queries, factor_panel, panel_other)
        pieces = call(
            solve_kernel, [shape(half, strip_rows)] * 4, [pltpu.VMEM((half, window), jnp.float32)], scalars=1
        )(where, ready, right_own, right_other, kept, swap(far, "side", 1))
        landed = [swap(pieces[step], "row", step) for step in (3, 2, 1)]
        own, other = call(
            sum_kernel, [shape(half // 2, strip_rows)] * 2, [pltpu.VMEM((half, strip_rows), jnp.float32)], scalars=1
        )(where, pieces[0], *landed)
        parts += [own, swap(other, "core", 1)]
        offset += cut
    return call(
        functools.partial(finish_kernel, QUERY_CUTS),
        shape(strip_rows, strip_cols),
        [pltpu.VMEM((strip_cols, strip_rows), jnp.float32)],
        scalars=1,
    )(where, *parts)


def shards_any(prev_solution, factor_panel, right_side, window_factor):
    row = lax.axis_index("row")
    strip_rows, strip_cols = right_side.shape
    by_rows = lax.all_to_all(prev_solution, ("row", "col"), split_axis=0, concat_axis=1, tiled=True)
    factor = lax.all_gather(window_factor, "row", axis=0, tiled=True)
    right = jnp.zeros((factor.shape[0], strip_cols), jnp.float32)
    right = lax.dynamic_update_slice_in_dim(right, right_side, row * strip_rows, 0)
    partial = exact(factor_panel, by_rows)
    coupling = lax.psum_scatter(partial, "col", scatter_dimension=1, tiled=True)
    solved = jax.scipy.linalg.solve_triangular(factor, right - coupling, lower=True)
    return lax.psum_scatter(solved, "row", scatter_dimension=0, tiled=True)


def solution(mesh):
    staged = mesh.shape["groups"] == 2 and mesh.shape["row"] == 4 and mesh.shape["col"] == 4
    if staged:
        mesh = Mesh(mesh.devices.reshape(2, 4, 2, 2), ("groups", "row", "side", "core"))
    col = ("side", "core") if staged else ("col",)
    in_specs = (P(None, ("groups", "row", *col)), P(None, ("row", *col)), P("row", ("groups", *col)), P("row", None))
    out_specs = P("row", ("groups", *col))
    body = shards if staged else shards_any
    return jax.shard_map(body, mesh=mesh, in_specs=in_specs, out_specs=out_specs, check_vma=False)
```

```python
import functools
import math

import jax
import jax.numpy as jnp
from jax import lax
from jax.experimental import pallas as pl
from jax.experimental.pallas import tpu as pltpu
from jax.sharding import Mesh
from jax.sharding import PartitionSpec as P

HIGHEST = lax.Precision.HIGHEST
SIZE = 128
VMEM = pl.BlockSpec(memory_space=pltpu.VMEM)
SMEM = pl.BlockSpec(memory_space=pltpu.SMEM)
QUERY_CUTS = (32,)


def exact(a, b):
    return jnp.dot(a, b, precision=HIGHEST, preferred_element_type=jnp.float32)


def near(a, b):
    a_high, a_low = halves(a)
    b_high, b_low = halves(b)
    total = jnp.dot(a_high, b_low, preferred_element_type=jnp.float32)
    total = total + jnp.dot(a_low, b_high, preferred_element_type=jnp.float32)
    return total + jnp.dot(a_high, b_high, preferred_element_type=jnp.float32)


def exact_t(a, b):
    return lax.dot_general(a, b, (((1,), (1,)), ((), ())), precision=HIGHEST, preferred_element_type=jnp.float32)


def call(kernel, outs, scratch=(), flops=10**6, scalars=0, spare=4):
    def run(*args):
        moved = sum(a.size * a.dtype.itemsize for a in args)
        held = sum(math.prod(a.shape) * a.dtype.itemsize for a in (*jax.tree.leaves(outs), *scratch))
        return pl.pallas_call(
            kernel,
            out_shape=outs,
            in_specs=[SMEM] * scalars + [VMEM] * (len(args) - scalars),
            out_specs=jax.tree.map(lambda _: VMEM, outs),
            scratch_shapes=list(scratch),
            cost_estimate=pl.CostEstimate(flops=flops, bytes_accessed=moved, transcendentals=0),
            compiler_params=pltpu.CompilerParams(vmem_limit_bytes=moved + held + spare * 2**20),
        )(*args)

    return run


def shape(*dims, dtype=jnp.float32):
    return jax.ShapeDtypeStruct(dims, dtype)


def rows_kernel(where_ref, share_ref, *refs):
    *landed_refs, near_ref, far_ref = refs
    half = near_ref.shape[2]
    for step, ref in enumerate((share_ref, *landed_refs)):
        near_ref[where_ref[0] ^ step] = ref[:, pl.ds(0, half)]
        far_ref[where_ref[0] ^ step] = ref[:, pl.ds(half, half)]


def first_kernel(where_ref, near_ref, near_other_ref, far_ref, far_other_ref, near_out, far_out):
    row, group, side, core = (where_ref[i] for i in range(4))
    near_out[side] = near_ref[...]
    near_out[1 - side] = near_other_ref[...]
    far_out[group] = far_ref[...]
    far_out[1 - group] = far_other_ref[...]


def second_kernel(where_ref, near_ref, near_other_ref, far_ref, far_other_ref, out_ref):
    row, group, side, core = (where_ref[i] for i in range(4))
    half = near_ref.shape[3]
    for r in range(4):
        for i in range(2):
            out_ref[r, group, i, :, pl.ds(0, half)] = near_ref[i, r]
            out_ref[r, 1 - group, i, :, pl.ds(0, half)] = near_other_ref[i, r]
            out_ref[r, i, side, :, pl.ds(half, half)] = far_ref[i, r]
            out_ref[r, i, 1 - side, :, pl.ds(half, half)] = far_other_ref[i, r]


def prepare_kernel(where_ref, own_ref, other_ref, ready_ref, factor_ref):
    core = where_ref[3]
    count = own_ref.shape[3]
    for piece in range(16):
        at = (piece // 4, piece // 2 % 2, piece % 2)
        for ref, index in ((own_ref, core), (other_ref, 1 - core)):
            start = pl.multiple_of((2 * piece + index) * count, 8)
            factor_ref[pl.ds(start, count), :] = ref[at]
    rows = lax.broadcasted_iota(jnp.int32, (SIZE, SIZE), 0)
    cols = lax.broadcasted_iota(jnp.int32, (SIZE, SIZE), 1)
    starts = range(0, factor_ref.shape[0], SIZE)
    blocks = [factor_ref[pl.ds(s, SIZE), pl.ds(s, SIZE)] for s in starts]
    inverses = []
    below = (rows % 2 == 1) & (cols == rows - 1)
    for block in blocks:
        lane = 1.0 / jnp.sum(jnp.where(rows == cols, block, 0.0), axis=0, keepdims=True)
        sublane = 1.0 / jnp.sum(jnp.where(rows == cols, block, 0.0), axis=1, keepdims=True)
        inverses.append(jnp.where(rows == cols, sublane, 0.0) - jnp.where(below, sublane * block * lane, 0.0))
    step = 2
    while step < SIZE:
        below = ((rows // step) % 2 == 1) & (cols // step == rows // step - 1)
        coupled = [near(jnp.where(below, b, 0.0), i) for b, i in zip(blocks, inverses)]
        inverses = [i - near(i, c) for i, c in zip(inverses, coupled)]
        step *= 2
    lower = [jnp.where(rows >= cols, block, 0.0) for block in blocks]
    errors = [jnp.where(rows == cols, 1.0, 0.0) - exact(b, i) for b, i in zip(lower, inverses)]
    inverses = [i + near(i, e) for i, e in zip(inverses, errors)]
    for start, inverse in zip(starts, inverses):
        if start:
            ready_ref[pl.ds(start, SIZE), pl.ds(0, start)] = exact(
                inverse, factor_ref[pl.ds(start, SIZE), pl.ds(0, start)]
            )
        ready_ref[pl.ds(start, SIZE), pl.ds(start, SIZE)] = inverse


def right_kernel(where_ref, right_ref, own_ref, other_ref, by_query):
    core = where_ref[3]
    by_query[...] = right_ref[...].T
    width = own_ref.shape[0] // 2
    for side in range(2):
        for ref, index in ((own_ref, core), (other_ref, 1 - core)):
            start = pl.multiple_of((2 * side + index) * width, 8)
            ref[pl.ds(side * width, width), :] = by_query[pl.ds(start, width), :]


def halves(value):
    high = value.astype(jnp.bfloat16)
    return high, (value - high.astype(jnp.float32)).astype(jnp.bfloat16)


def split_kernel(where_ref, queries_ref, high_ref, low_ref):
    side, core = where_ref[2], where_ref[3]
    count, columns = queries_ref.shape[0] // 2, queries_ref.shape[1] // 2
    for part in range(2):
        rows = pl.ds(pl.multiple_of(((side + part) % 2) * count, 8), count)
        for half in range(2):
            cols = pl.ds(pl.multiple_of(((core + half) % 2) * columns, 128), columns)
            here = (pl.ds(part * count, count), pl.ds(half * columns, columns))
            high_ref[here], low_ref[here] = halves(queries_ref[rows, cols])


def multiply(high_ref, low_ref, panel_refs, kept_ref, far_ref):
    count, window = kept_ref.shape
    columns = panel_refs[0].shape[1]

    def product(a, b):
        return lax.dot_general(a, b, (((1,), (1,)), ((), ())), preferred_element_type=jnp.float32)

    for start in range(0, window, 256):
        here = pl.ds(start, 256)
        total = 0.0
        for half, ref in enumerate(panel_refs):
            cols = pl.ds(half * columns, columns)
            high, low = halves(ref[here, :])
            total = total + product(high_ref[:, cols], high)
            total = total + product(low_ref[:, cols], high) + product(high_ref[:, cols], low)
        kept_ref[:, here] = total[:count]
        far_ref[:, here] = total[count:]


def couple_kernel(where_ref, queries_ref, own_ref, other_ref, kept_ref, far_ref, high_ref, low_ref):
    split_kernel(where_ref, queries_ref, high_ref, low_ref)
    multiply(high_ref, low_ref, (own_ref, other_ref), kept_ref, far_ref)


def couple_more_kernel(high_ref, low_ref, own_ref, other_ref, kept_ref, far_ref):
    multiply(high_ref, low_ref, (own_ref, other_ref), kept_ref, far_ref)


def deal_kernel(queries_ref, *out_refs):
    columns = out_refs[0].shape[2]
    offset = 0
    for out_ref in out_refs:
        for chip in range(8):
            out_ref[chip] = queries_ref[pl.ds(offset, out_ref.shape[1]), pl.ds(chip * columns, columns)]
        offset += out_ref.shape[1]


def solve_part(base, where_ref, ready_ref, right_refs, kept_ref, arrived_ref, left):
    count, strip = right_refs[0].shape
    rows = kept_ref.shape[1]
    row, core = where_ref[0], where_ref[3]
    part = pl.ds(base, rows)
    left[:, part] = -(kept_ref[...] + arrived_ref[...])

    @pl.when(row // (rows // strip) == base // rows)
    def _():
        cols = pl.ds(pl.multiple_of(row * strip, strip), strip)
        for ref, index in zip(right_refs, (core, 1 - core)):
            here = (pl.ds(pl.multiple_of(index * count, 8), count), cols)
            left[here] = left[here] + ref[...]

    for start in range(base, base + rows, SIZE):
        here = pl.ds(start, SIZE)
        left[:, here] = exact_t(left[:, here], ready_ref[here, here])
    if base:
        solved = pl.ds(0, base)
        left[:, part] = left[:, part] - exact_t(left[:, solved], ready_ref[part, solved])
    for start in range(base, base + rows, 2 * SIZE):
        first, second = pl.ds(start, SIZE), pl.ds(start + SIZE, SIZE)
        left[:, second] = left[:, second] - exact_t(left[:, first], ready_ref[second, first])
        below = pl.ds(start + 2 * SIZE, base + rows - start - 2 * SIZE)
        if below.size:
            both = pl.ds(start, 2 * SIZE)
            left[:, below] = left[:, below] - exact_t(left[:, both], ready_ref[below, both])


def solve_first_kernel(where_ref, ready_ref, right_own_ref, right_other_ref, kept_ref, arrived_ref, solved_ref):
    solve_part(0, where_ref, ready_ref, (right_own_ref, right_other_ref), kept_ref, arrived_ref, solved_ref)


def solve_second_kernel(
    where_ref, ready_ref, right_own_ref, right_other_ref, solved_ref, kept_ref, arrived_ref, *out_refs
):
    *piece_refs, left = out_refs
    strip = right_own_ref.shape[1]
    base = solved_ref.shape[1]
    left[:, pl.ds(0, base)] = solved_ref[...]
    solve_part(base, where_ref, ready_ref, (right_own_ref, right_other_ref), kept_ref, arrived_ref, left)
    for step, piece_ref in enumerate(piece_refs):
        piece_ref[...] = left[:, pl.ds(pl.multiple_of((where_ref[0] ^ step) * strip, strip), strip)]


def sum_kernel(where_ref, *refs):
    *piece_refs, own_ref, other_ref, total = refs
    value = piece_refs[0][...]
    for ref in piece_refs[1:]:
        value = value + ref[...]
    total[...] = value
    count = own_ref.shape[0]
    own_ref[...] = total[pl.ds(pl.multiple_of(where_ref[3] * count, 8), count), :]
    other_ref[...] = total[pl.ds(pl.multiple_of((1 - where_ref[3]) * count, 8), count), :]


def finish_kernel(cuts, where_ref, *refs):
    *part_refs, out_ref, total = refs
    offset = 0
    width = sum(cuts)
    for cut, own_ref, other_ref in zip(cuts, part_refs[::2], part_refs[1::2]):
        for ref, core in ((own_ref, where_ref[3]), (other_ref, 1 - where_ref[3])):
            for side in range(2):
                place = pl.multiple_of(side * 2 * width + core * width + offset, 8)
                total[pl.ds(place, cut), :] = ref[pl.ds(side * cut, cut), :]
        offset += cut
    out_ref[...] = total[...].T


def swap(value, axis, step):
    return lax.ppermute(value, axis, [(i, i ^ step) for i in range(lax.axis_size(axis))])


def shards(prev_solution, factor_panel, right_side, window_factor):
    row, group, side, core = (lax.axis_index(a) for a in ("row", "groups", "side", "core"))
    where = jnp.stack([row, group, side, core])
    strip_rows, strip_cols = right_side.shape
    window = window_factor.shape[1]
    width = prev_solution.shape[1]
    share_rows, half_window = strip_rows // 8, window // 2

    share = lax.dynamic_slice_in_dim(window_factor, (group * 4 + side * 2 + core) * share_rows, share_rows, 0)
    landed = [swap(share, "row", step) for step in (1, 2, 3)]
    right_own, right_other = call(
        right_kernel,
        [shape(2 * width, strip_rows)] * 2,
        [pltpu.VMEM((strip_cols, strip_rows), jnp.float32)],
        flops=5 * 10**10,
        scalars=1,
    )(where, right_side)
    panels = [factor_panel[:half_window], factor_panel[half_window:]]
    others = [swap(panel, "core", 1) for panel in panels]
    landed, right_own = lax.optimization_barrier((landed, right_own))
    right_other = swap(right_other, "core", 1)
    near, far = call(rows_kernel, [shape(4, share_rows, half_window)] * 2, scalars=1)(where, share, *landed)
    near, far = call(first_kernel, [shape(2, 4, share_rows, half_window)] * 2, scalars=1)(
        where, near, swap(near, "side", 1), far, swap(far, "groups", 1)
    )
    near, others, right_other = lax.optimization_barrier((near, others, right_other))
    shares = call(second_kernel, shape(4, 2, 2, share_rows, window), scalars=1)(
        where, near, swap(near, "groups", 1), far, swap(far, "side", 1)
    )

    dealt = call(deal_kernel, [shape(8, cut, 2 * factor_panel.shape[1]) for cut in QUERY_CUTS])(prev_solution.T)
    offset = 0
    parts = []
    for number, cut in enumerate(QUERY_CUTS):
        queries = lax.all_to_all(dealt[number], ("row", "side"), split_axis=0, concat_axis=0, tiled=True)
        queries = queries.reshape(8 * cut, -1)
        half = 4 * cut
        if not offset:
            queries, shares = lax.optimization_barrier((queries, shares))
        kept, far, high, low = call(
            couple_kernel,
            [shape(half, half_window)] * 2 + [shape(*queries.shape, dtype=jnp.bfloat16)] * 2,
            scalars=1,
        )(where, queries, panels[0], others[0])
        if not offset:
            far, shares = lax.optimization_barrier((far, shares))
            ready = call(
                prepare_kernel, shape(window, window), [pltpu.VMEM((window, window), jnp.float32)], scalars=1
            )(where, shares, swap(shares, "core", 1))
        kept_more, far_more = call(couple_more_kernel, [shape(half, half_window)] * 2)(high, low, panels[1], others[1])
        rights = (right_own, right_other)
        solved = call(solve_first_kernel, shape(half, half_window), scalars=1)(
            where, ready, *rights, kept, swap(far, "side", 1)
        )
        pieces = call(
            solve_second_kernel, [shape(half, strip_rows)] * 4, [pltpu.VMEM((half, window), jnp.float32)], scalars=1
        )(where, ready, *rights, solved, kept_more, swap(far_more, "side", 1))
        landed = [swap(pieces[step], "row", step) for step in (3, 2, 1)]
        own, other = call(
            sum_kernel, [shape(half // 2, strip_rows)] * 2, [pltpu.VMEM((half, strip_rows), jnp.float32)], scalars=1
        )(where, pieces[0], *landed)
        parts += [own, swap(other, "core", 1)]
        offset += cut
    return call(
        functools.partial(finish_kernel, QUERY_CUTS),
        shape(strip_rows, strip_cols),
        [pltpu.VMEM((strip_cols, strip_rows), jnp.float32)],
        scalars=1,
    )(where, *parts)


def shards_any(prev_solution, factor_panel, right_side, window_factor):
    row = lax.axis_index("row")
    strip_rows, strip_cols = right_side.shape
    by_rows = lax.all_to_all(prev_solution, ("row", "col"), split_axis=0, concat_axis=1, tiled=True)
    factor = lax.all_gather(window_factor, "row", axis=0, tiled=True)
    right = jnp.zeros((factor.shape[0], strip_cols), jnp.float32)
    right = lax.dynamic_update_slice_in_dim(right, right_side, row * strip_rows, 0)
    partial = exact(factor_panel, by_rows)
    coupling = lax.psum_scatter(partial, "col", scatter_dimension=1, tiled=True)
    solved = jax.scipy.linalg.solve_triangular(factor, right - coupling, lower=True)
    return lax.psum_scatter(solved, "row", scatter_dimension=0, tiled=True)


def solution(mesh):
    staged = mesh.shape["groups"] == 2 and mesh.shape["row"] == 4 and mesh.shape["col"] == 4
    if staged:
        mesh = Mesh(mesh.devices.reshape(2, 4, 2, 2), ("groups", "row", "side", "core"))
    col = ("side", "core") if staged else ("col",)
    in_specs = (P(None, ("groups", "row", *col)), P(None, ("row", *col)), P("row", ("groups", *col)), P("row", None))
    out_specs = P("row", ("groups", *col))
    body = shards if staged else shards_any
    return jax.shard_map(body, mesh=mesh, in_specs=in_specs, out_specs=out_specs, check_vma=False)
```

```python
import functools
import math

import jax
import jax.numpy as jnp
from jax import lax
from jax.experimental import pallas as pl
from jax.experimental.pallas import tpu as pltpu
from jax.sharding import Mesh
from jax.sharding import PartitionSpec as P

HIGHEST = lax.Precision.HIGHEST
SIZE = 128
VMEM = pl.BlockSpec(memory_space=pltpu.VMEM)
SMEM = pl.BlockSpec(memory_space=pltpu.SMEM)
QUERY_CUTS = (32,)


def exact(a, b):
    return jnp.dot(a, b, precision=HIGHEST, preferred_element_type=jnp.float32)


def near(a, b):
    a_high, a_low = halves(a)
    b_high, b_low = halves(b)
    total = jnp.dot(a_high, b_low, preferred_element_type=jnp.float32)
    total = total + jnp.dot(a_low, b_high, preferred_element_type=jnp.float32)
    return total + jnp.dot(a_high, b_high, preferred_element_type=jnp.float32)


def exact_t(a, b):
    return lax.dot_general(a, b, (((1,), (1,)), ((), ())), precision=HIGHEST, preferred_element_type=jnp.float32)


def call(kernel, outs, scratch=(), flops=10**6, scalars=0, spare=4):
    def run(*args):
        moved = sum(a.size * a.dtype.itemsize for a in args)
        held = sum(math.prod(a.shape) * a.dtype.itemsize for a in (*jax.tree.leaves(outs), *scratch))
        return pl.pallas_call(
            kernel,
            out_shape=outs,
            in_specs=[SMEM] * scalars + [VMEM] * (len(args) - scalars),
            out_specs=jax.tree.map(lambda _: VMEM, outs),
            scratch_shapes=list(scratch),
            cost_estimate=pl.CostEstimate(flops=flops, bytes_accessed=moved, transcendentals=0),
            compiler_params=pltpu.CompilerParams(vmem_limit_bytes=moved + held + spare * 2**20),
        )(*args)

    return run


def shape(*dims, dtype=jnp.float32):
    return jax.ShapeDtypeStruct(dims, dtype)


def rows_kernel(where_ref, share_ref, *refs):
    *landed_refs, near_ref, far_ref = refs
    half = near_ref.shape[2]
    for step, ref in enumerate((share_ref, *landed_refs)):
        source = where_ref[0] ^ step
        near_ref[source] = ref[:, pl.ds(0, half)]

        @pl.when(source >= 2)
        def _(source=source, ref=ref):
            far_ref[source - 2] = ref[:, pl.ds(half, half)]


def first_kernel(where_ref, near_ref, near_other_ref, far_ref, far_other_ref, near_out, far_out):
    row, group, side, core = (where_ref[i] for i in range(4))
    near_out[side] = near_ref[...]
    near_out[1 - side] = near_other_ref[...]
    far_out[group] = far_ref[...]
    far_out[1 - group] = far_other_ref[...]


def second_kernel(where_ref, near_ref, near_other_ref, far_ref, far_other_ref, out_ref):
    row, group, side, core = (where_ref[i] for i in range(4))
    half = near_ref.shape[3]
    for r in range(4):
        for i in range(2):
            out_ref[r, group, i, :, pl.ds(0, half)] = near_ref[i, r]
            out_ref[r, 1 - group, i, :, pl.ds(0, half)] = near_other_ref[i, r]
            if r < 2:
                out_ref[r, i, :, :, pl.ds(half, half)] = jnp.zeros((2, *near_ref.shape[2:]), jnp.float32)
            else:
                out_ref[r, i, side, :, pl.ds(half, half)] = far_ref[i, r - 2]
                out_ref[r, i, 1 - side, :, pl.ds(half, half)] = far_other_ref[i, r - 2]


def prepare_kernel(where_ref, own_ref, other_ref, ready_ref, factor_ref):
    core = where_ref[3]
    count = own_ref.shape[3]
    for piece in range(16):
        at = (piece // 4, piece // 2 % 2, piece % 2)
        for ref, index in ((own_ref, core), (other_ref, 1 - core)):
            start = pl.multiple_of((2 * piece + index) * count, 8)
            factor_ref[pl.ds(start, count), :] = ref[at]
    rows = lax.broadcasted_iota(jnp.int32, (SIZE, SIZE), 0)
    cols = lax.broadcasted_iota(jnp.int32, (SIZE, SIZE), 1)
    starts = range(0, factor_ref.shape[0], SIZE)
    blocks = [factor_ref[pl.ds(s, SIZE), pl.ds(s, SIZE)] for s in starts]
    inverses = []
    below = (rows % 2 == 1) & (cols == rows - 1)
    for block in blocks:
        lane = 1.0 / jnp.sum(jnp.where(rows == cols, block, 0.0), axis=0, keepdims=True)
        sublane = 1.0 / jnp.sum(jnp.where(rows == cols, block, 0.0), axis=1, keepdims=True)
        inverses.append(jnp.where(rows == cols, sublane, 0.0) - jnp.where(below, sublane * block * lane, 0.0))
    step = 2
    while step < SIZE:
        below = ((rows // step) % 2 == 1) & (cols // step == rows // step - 1)
        coupled = [near(jnp.where(below, b, 0.0), i) for b, i in zip(blocks, inverses)]
        inverses = [i - near(i, c) for i, c in zip(inverses, coupled)]
        step *= 2
    lower = [jnp.where(rows >= cols, block, 0.0) for block in blocks]
    errors = [jnp.where(rows == cols, 1.0, 0.0) - exact(b, i) for b, i in zip(lower, inverses)]
    inverses = [i + near(i, e) for i, e in zip(inverses, errors)]
    for start, inverse in zip(starts, inverses):
        if start:
            ready_ref[pl.ds(start, SIZE), pl.ds(0, start)] = exact(
                inverse, factor_ref[pl.ds(start, SIZE), pl.ds(0, start)]
            )
        ready_ref[pl.ds(start, SIZE), pl.ds(start, SIZE)] = inverse


def right_kernel(where_ref, right_ref, own_ref, other_ref, by_query):
    core = where_ref[3]
    by_query[...] = right_ref[...].T
    width = own_ref.shape[0] // 2
    for side in range(2):
        for ref, index in ((own_ref, core), (other_ref, 1 - core)):
            start = pl.multiple_of((2 * side + index) * width, 8)
            ref[pl.ds(side * width, width), :] = by_query[pl.ds(start, width), :]


def halves(value):
    high = value.astype(jnp.bfloat16)
    return high, (value - high.astype(jnp.float32)).astype(jnp.bfloat16)


def split_kernel(where_ref, queries_ref, high_ref, low_ref):
    side, core = where_ref[2], where_ref[3]
    count, columns = queries_ref.shape[0] // 2, queries_ref.shape[1] // 2
    for part in range(2):
        rows = pl.ds(pl.multiple_of(((side + part) % 2) * count, 8), count)
        for half in range(2):
            cols = pl.ds(pl.multiple_of(((core + half) % 2) * columns, 128), columns)
            here = (pl.ds(part * count, count), pl.ds(half * columns, columns))
            high_ref[here], low_ref[here] = halves(queries_ref[rows, cols])


def multiply(high_ref, low_ref, panel_refs, kept_ref, far_ref):
    count, window = kept_ref.shape
    columns = panel_refs[0].shape[1]

    def product(a, b):
        return lax.dot_general(a, b, (((1,), (1,)), ((), ())), preferred_element_type=jnp.float32)

    for start in range(0, window, 256):
        here = pl.ds(start, 256)
        total = 0.0
        for half, ref in enumerate(panel_refs):
            cols = pl.ds(half * columns, columns)
            high, low = halves(ref[here, :])
            total = total + product(high_ref[:, cols], high)
            total = total + product(low_ref[:, cols], high) + product(high_ref[:, cols], low)
        kept_ref[:, here] = total[:count]
        far_ref[:, here] = total[count:]


def couple_kernel(where_ref, queries_ref, own_ref, other_ref, kept_ref, far_ref, high_ref, low_ref):
    split_kernel(where_ref, queries_ref, high_ref, low_ref)
    multiply(high_ref, low_ref, (own_ref, other_ref), kept_ref, far_ref)


def couple_more_kernel(high_ref, low_ref, own_ref, other_ref, kept_ref, far_ref):
    multiply(high_ref, low_ref, (own_ref, other_ref), kept_ref, far_ref)


def deal_kernel(queries_ref, *out_refs):
    columns = out_refs[0].shape[2]
    offset = 0
    for out_ref in out_refs:
        for chip in range(8):
            out_ref[chip] = queries_ref[pl.ds(offset, out_ref.shape[1]), pl.ds(chip * columns, columns)]
        offset += out_ref.shape[1]


def solve_part(base, where_ref, ready_ref, right_refs, kept_ref, arrived_ref, left):
    count, strip = right_refs[0].shape
    rows = kept_ref.shape[1]
    row, core = where_ref[0], where_ref[3]
    part = pl.ds(base, rows)
    left[:, part] = -(kept_ref[...] + arrived_ref[...])

    @pl.when(row // (rows // strip) == base // rows)
    def _():
        cols = pl.ds(pl.multiple_of(row * strip, strip), strip)
        for ref, index in zip(right_refs, (core, 1 - core)):
            here = (pl.ds(pl.multiple_of(index * count, 8), count), cols)
            left[here] = left[here] + ref[...]

    for start in range(base, base + rows, SIZE):
        here = pl.ds(start, SIZE)
        left[:, here] = exact_t(left[:, here], ready_ref[here, here])
    if base:
        solved = pl.ds(0, base)
        left[:, part] = left[:, part] - exact_t(left[:, solved], ready_ref[part, solved])
    for start in range(base, base + rows, 2 * SIZE):
        first, second = pl.ds(start, SIZE), pl.ds(start + SIZE, SIZE)
        left[:, second] = left[:, second] - exact_t(left[:, first], ready_ref[second, first])
        below = pl.ds(start + 2 * SIZE, base + rows - start - 2 * SIZE)
        if below.size:
            both = pl.ds(start, 2 * SIZE)
            left[:, below] = left[:, below] - exact_t(left[:, both], ready_ref[below, both])


def solve_first_kernel(where_ref, ready_ref, right_own_ref, right_other_ref, kept_ref, arrived_ref, solved_ref):
    solve_part(0, where_ref, ready_ref, (right_own_ref, right_other_ref), kept_ref, arrived_ref, solved_ref)


def solve_second_kernel(
    where_ref, ready_ref, right_own_ref, right_other_ref, solved_ref, kept_ref, arrived_ref, *out_refs
):
    *piece_refs, left = out_refs
    strip = right_own_ref.shape[1]
    base = solved_ref.shape[1]
    left[:, pl.ds(0, base)] = solved_ref[...]
    solve_part(base, where_ref, ready_ref, (right_own_ref, right_other_ref), kept_ref, arrived_ref, left)
    for step, piece_ref in enumerate(piece_refs):
        piece_ref[...] = left[:, pl.ds(pl.multiple_of((where_ref[0] ^ step) * strip, strip), strip)]


def sum_kernel(where_ref, *refs):
    *piece_refs, own_ref, other_ref, total = refs
    value = piece_refs[0][...]
    for ref in piece_refs[1:]:
        value = value + ref[...]
    total[...] = value
    count = own_ref.shape[0]
    own_ref[...] = total[pl.ds(pl.multiple_of(where_ref[3] * count, 8), count), :]
    other_ref[...] = total[pl.ds(pl.multiple_of((1 - where_ref[3]) * count, 8), count), :]


def finish_kernel(cuts, where_ref, *refs):
    *part_refs, out_ref, total = refs
    offset = 0
    width = sum(cuts)
    for cut, own_ref, other_ref in zip(cuts, part_refs[::2], part_refs[1::2]):
        for ref, core in ((own_ref, where_ref[3]), (other_ref, 1 - where_ref[3])):
            for side in range(2):
                place = pl.multiple_of(side * 2 * width + core * width + offset, 8)
                total[pl.ds(place, cut), :] = ref[pl.ds(side * cut, cut), :]
        offset += cut
    out_ref[...] = total[...].T


def swap(value, axis, step):
    return lax.ppermute(value, axis, [(i, i ^ step) for i in range(lax.axis_size(axis))])


def shards(prev_solution, factor_panel, right_side, window_factor):
    row, group, side, core = (lax.axis_index(a) for a in ("row", "groups", "side", "core"))
    where = jnp.stack([row, group, side, core])
    strip_rows, strip_cols = right_side.shape
    window = window_factor.shape[1]
    width = prev_solution.shape[1]
    share_rows, half_window = strip_rows // 8, window // 2

    share = lax.dynamic_slice_in_dim(window_factor, (group * 4 + side * 2 + core) * share_rows, share_rows, 0)
    landed = [swap(share, "row", step) for step in (1, 2, 3)]
    right_own, right_other = call(
        right_kernel,
        [shape(2 * width, strip_rows)] * 2,
        [pltpu.VMEM((strip_cols, strip_rows), jnp.float32)],
        flops=5 * 10**10,
        scalars=1,
    )(where, right_side)
    panels = [factor_panel[:half_window], factor_panel[half_window:]]
    others = [swap(panel, "core", 1) for panel in panels]
    landed, right_own = lax.optimization_barrier((landed, right_own))
    right_other = swap(right_other, "core", 1)
    sizes = [shape(4, share_rows, half_window), shape(2, share_rows, half_window)]
    near, far = call(rows_kernel, sizes, scalars=1)(where, share, *landed)
    near, far = call(first_kernel, [shape(2, *size.shape) for size in sizes], scalars=1)(
        where, near, swap(near, "side", 1), far, swap(far, "groups", 1)
    )
    near, others, right_other = lax.optimization_barrier((near, others, right_other))
    shares = call(second_kernel, shape(4, 2, 2, share_rows, window), scalars=1)(
        where, near, swap(near, "groups", 1), far, swap(far, "side", 1)
    )

    dealt = call(deal_kernel, [shape(8, cut, 2 * factor_panel.shape[1]) for cut in QUERY_CUTS])(prev_solution.T)
    offset = 0
    parts = []
    for number, cut in enumerate(QUERY_CUTS):
        queries = lax.all_to_all(dealt[number], ("row", "side"), split_axis=0, concat_axis=0, tiled=True)
        queries = queries.reshape(8 * cut, -1)
        half = 4 * cut
        if not offset:
            queries, shares = lax.optimization_barrier((queries, shares))
        kept, far, high, low = call(
            couple_kernel,
            [shape(half, half_window)] * 2 + [shape(*queries.shape, dtype=jnp.bfloat16)] * 2,
            scalars=1,
        )(where, queries, panels[0], others[0])
        if not offset:
            far, shares = lax.optimization_barrier((far, shares))
            ready = call(
                prepare_kernel, shape(window, window), [pltpu.VMEM((window, window), jnp.float32)], scalars=1
            )(where, shares, swap(shares, "core", 1))
        kept_more, far_more = call(couple_more_kernel, [shape(half, half_window)] * 2)(high, low, panels[1], others[1])
        rights = (right_own, right_other)
        solved = call(solve_first_kernel, shape(half, half_window), scalars=1)(
            where, ready, *rights, kept, swap(far, "side", 1)
        )
        pieces = call(
            solve_second_kernel, [shape(half, strip_rows)] * 4, [pltpu.VMEM((half, window), jnp.float32)], scalars=1
        )(where, ready, *rights, solved, kept_more, swap(far_more, "side", 1))
        landed = [swap(pieces[step], "row", step) for step in (3, 2, 1)]
        own, other = call(
            sum_kernel, [shape(half // 2, strip_rows)] * 2, [pltpu.VMEM((half, strip_rows), jnp.float32)], scalars=1
        )(where, pieces[0], *landed)
        parts += [own, swap(other, "core", 1)]
        offset += cut
    return call(
        functools.partial(finish_kernel, QUERY_CUTS),
        shape(strip_rows, strip_cols),
        [pltpu.VMEM((strip_cols, strip_rows), jnp.float32)],
        scalars=1,
    )(where, *parts)


def shards_any(prev_solution, factor_panel, right_side, window_factor):
    row = lax.axis_index("row")
    strip_rows, strip_cols = right_side.shape
    by_rows = lax.all_to_all(prev_solution, ("row", "col"), split_axis=0, concat_axis=1, tiled=True)
    factor = lax.all_gather(window_factor, "row", axis=0, tiled=True)
    right = jnp.zeros((factor.shape[0], strip_cols), jnp.float32)
    right = lax.dynamic_update_slice_in_dim(right, right_side, row * strip_rows, 0)
    partial = exact(factor_panel, by_rows)
    coupling = lax.psum_scatter(partial, "col", scatter_dimension=1, tiled=True)
    solved = jax.scipy.linalg.solve_triangular(factor, right - coupling, lower=True)
    return lax.psum_scatter(solved, "row", scatter_dimension=0, tiled=True)


def solution(mesh):
    staged = mesh.shape["groups"] == 2 and mesh.shape["row"] == 4 and mesh.shape["col"] == 4
    if staged:
        mesh = Mesh(mesh.devices.reshape(2, 4, 2, 2), ("groups", "row", "side", "core"))
    col = ("side", "core") if staged else ("col",)
    in_specs = (P(None, ("groups", "row", *col)), P(None, ("row", *col)), P("row", ("groups", *col)), P("row", None))
    out_specs = P("row", ("groups", *col))
    body = shards if staged else shards_any
    return jax.shard_map(body, mesh=mesh, in_specs=in_specs, out_specs=out_specs, check_vma=False)
```

```python
import functools
import math

import jax
import jax.numpy as jnp
from jax import lax
from jax.experimental import pallas as pl
from jax.experimental.pallas import tpu as pltpu
from jax.sharding import Mesh
from jax.sharding import PartitionSpec as P

HIGHEST = lax.Precision.HIGHEST
SIZE = 128
VMEM = pl.BlockSpec(memory_space=pltpu.VMEM)
SMEM = pl.BlockSpec(memory_space=pltpu.SMEM)
QUERY_CUTS = (32,)


def exact(a, b):
    return jnp.dot(a, b, precision=HIGHEST, preferred_element_type=jnp.float32)


def near(a, b):
    a_high, a_low = halves(a)
    b_high, b_low = halves(b)
    total = jnp.dot(a_high, b_low, preferred_element_type=jnp.float32)
    total = total + jnp.dot(a_low, b_high, preferred_element_type=jnp.float32)
    return total + jnp.dot(a_high, b_high, preferred_element_type=jnp.float32)


def exact_t(a, b):
    return lax.dot_general(a, b, (((1,), (1,)), ((), ())), precision=HIGHEST, preferred_element_type=jnp.float32)


def call(kernel, outs, scratch=(), flops=10**6, scalars=0, spare=4):
    def run(*args):
        moved = sum(a.size * a.dtype.itemsize for a in args)
        held = sum(math.prod(a.shape) * a.dtype.itemsize for a in (*jax.tree.leaves(outs), *scratch))
        return pl.pallas_call(
            kernel,
            out_shape=outs,
            in_specs=[SMEM] * scalars + [VMEM] * (len(args) - scalars),
            out_specs=jax.tree.map(lambda _: VMEM, outs),
            scratch_shapes=list(scratch),
            cost_estimate=pl.CostEstimate(flops=flops, bytes_accessed=moved, transcendentals=0),
            compiler_params=pltpu.CompilerParams(vmem_limit_bytes=moved + held + spare * 2**20),
        )(*args)

    return run


def shape(*dims, dtype=jnp.float32):
    return jax.ShapeDtypeStruct(dims, dtype)


def rows_kernel(where_ref, share_ref, *refs):
    *landed_refs, near_ref, far_ref = refs
    width = near_ref.shape[2]
    for step, ref in enumerate((share_ref, *landed_refs)):
        source = where_ref[0] ^ step
        near_ref[source] = ref[:, pl.ds(0, width)]
        for quarter, out_ref, first in ((1, near_ref, 3), (2, far_ref, -2), (3, far_ref, -1)):

            @pl.when(source >= quarter)
            def _(source=source, ref=ref, quarter=quarter, out_ref=out_ref, first=first):
                out_ref[source + first] = ref[:, pl.ds(quarter * width, width)]


def first_kernel(where_ref, near_ref, near_other_ref, far_ref, far_other_ref, near_out, far_out):
    row, group, side, core = (where_ref[i] for i in range(4))
    near_out[side] = near_ref[...]
    near_out[1 - side] = near_other_ref[...]
    far_out[group] = far_ref[...]
    far_out[1 - group] = far_other_ref[...]


def second_kernel(where_ref, near_ref, near_other_ref, far_ref, far_other_ref, out_ref):
    row, group, side, core = (where_ref[i] for i in range(4))
    width = near_ref.shape[3]
    zero = jnp.zeros(near_ref.shape[2:], jnp.float32)
    for r in range(4):
        for i in range(2):
            for quarter, first in enumerate((0, 3, -2, -1)):
                cols = pl.ds(quarter * width, width)
                if quarter < 2:
                    here, other = out_ref.at[r, group, i, :, cols], out_ref.at[r, 1 - group, i, :, cols]
                    refs = near_ref, near_other_ref
                else:
                    here, other = out_ref.at[r, i, side, :, cols], out_ref.at[r, i, 1 - side, :, cols]
                    refs = far_ref, far_other_ref
                here[...] = refs[0][i, r + first] if r >= quarter else zero
                other[...] = refs[1][i, r + first] if r >= quarter else zero


def prepare_kernel(where_ref, own_ref, other_ref, ready_ref, factor_ref):
    core = where_ref[3]
    count = own_ref.shape[3]
    for piece in range(16):
        at = (piece // 4, piece // 2 % 2, piece % 2)
        for ref, index in ((own_ref, core), (other_ref, 1 - core)):
            start = pl.multiple_of((2 * piece + index) * count, 8)
            factor_ref[pl.ds(start, count), :] = ref[at]
    rows = lax.broadcasted_iota(jnp.int32, (SIZE, SIZE), 0)
    cols = lax.broadcasted_iota(jnp.int32, (SIZE, SIZE), 1)
    starts = range(0, factor_ref.shape[0], SIZE)
    blocks = [factor_ref[pl.ds(s, SIZE), pl.ds(s, SIZE)] for s in starts]
    inverses = []
    below = (rows % 2 == 1) & (cols == rows - 1)
    for block in blocks:
        lane = 1.0 / jnp.sum(jnp.where(rows == cols, block, 0.0), axis=0, keepdims=True)
        sublane = 1.0 / jnp.sum(jnp.where(rows == cols, block, 0.0), axis=1, keepdims=True)
        inverses.append(jnp.where(rows == cols, sublane, 0.0) - jnp.where(below, sublane * block * lane, 0.0))
    step = 2
    while step < SIZE:
        below = ((rows // step) % 2 == 1) & (cols // step == rows // step - 1)
        coupled = [near(jnp.where(below, b, 0.0), i) for b, i in zip(blocks, inverses)]
        inverses = [i - near(i, c) for i, c in zip(inverses, coupled)]
        step *= 2
    lower = [jnp.where(rows >= cols, block, 0.0) for block in blocks]
    errors = [jnp.where(rows == cols, 1.0, 0.0) - exact(b, i) for b, i in zip(lower, inverses)]
    inverses = [i + near(i, e) for i, e in zip(inverses, errors)]
    for start, inverse in zip(starts, inverses):
        if start:
            ready_ref[pl.ds(start, SIZE), pl.ds(0, start)] = exact(
                inverse, factor_ref[pl.ds(start, SIZE), pl.ds(0, start)]
            )
        ready_ref[pl.ds(start, SIZE), pl.ds(start, SIZE)] = inverse


def right_kernel(where_ref, right_ref, own_ref, other_ref, by_query):
    core = where_ref[3]
    by_query[...] = right_ref[...].T
    width = own_ref.shape[0] // 2
    for side in range(2):
        for ref, index in ((own_ref, core), (other_ref, 1 - core)):
            start = pl.multiple_of((2 * side + index) * width, 8)
            ref[pl.ds(side * width, width), :] = by_query[pl.ds(start, width), :]


def halves(value):
    high = value.astype(jnp.bfloat16)
    return high, (value - high.astype(jnp.float32)).astype(jnp.bfloat16)


def split_kernel(where_ref, queries_ref, high_ref, low_ref):
    side, core = where_ref[2], where_ref[3]
    count, columns = queries_ref.shape[0] // 2, queries_ref.shape[1] // 2
    for part in range(2):
        rows = pl.ds(pl.multiple_of(((side + part) % 2) * count, 8), count)
        for half in range(2):
            cols = pl.ds(pl.multiple_of(((core + half) % 2) * columns, 128), columns)
            here = (pl.ds(part * count, count), pl.ds(half * columns, columns))
            high_ref[here], low_ref[here] = halves(queries_ref[rows, cols])


def multiply(high_ref, low_ref, panel_refs, kept_ref, far_ref):
    count, window = kept_ref.shape
    columns = panel_refs[0].shape[1]

    def product(a, b):
        return lax.dot_general(a, b, (((1,), (1,)), ((), ())), preferred_element_type=jnp.float32)

    for start in range(0, window, 256):
        here = pl.ds(start, 256)
        total = 0.0
        for half, ref in enumerate(panel_refs):
            cols = pl.ds(half * columns, columns)
            high, low = halves(ref[here, :])
            total = total + product(high_ref[:, cols], high)
            total = total + product(low_ref[:, cols], high) + product(high_ref[:, cols], low)
        kept_ref[:, here] = total[:count]
        far_ref[:, here] = total[count:]


def couple_kernel(where_ref, queries_ref, own_ref, other_ref, kept_ref, far_ref, high_ref, low_ref):
    split_kernel(where_ref, queries_ref, high_ref, low_ref)
    multiply(high_ref, low_ref, (own_ref, other_ref), kept_ref, far_ref)


def couple_more_kernel(high_ref, low_ref, own_ref, other_ref, kept_ref, far_ref):
    multiply(high_ref, low_ref, (own_ref, other_ref), kept_ref, far_ref)


def deal_kernel(queries_ref, *out_refs):
    columns = out_refs[0].shape[2]
    offset = 0
    for out_ref in out_refs:
        for chip in range(8):
            out_ref[chip] = queries_ref[pl.ds(offset, out_ref.shape[1]), pl.ds(chip * columns, columns)]
        offset += out_ref.shape[1]


def solve_part(base, where_ref, ready_ref, right_refs, kept_ref, arrived_ref, left):
    count, strip = right_refs[0].shape
    rows = kept_ref.shape[1]
    row, core = where_ref[0], where_ref[3]
    part = pl.ds(base, rows)
    left[:, part] = -(kept_ref[...] + arrived_ref[...])

    @pl.when(row // (rows // strip) == base // rows)
    def _():
        cols = pl.ds(pl.multiple_of(row * strip, strip), strip)
        for ref, index in zip(right_refs, (core, 1 - core)):
            here = (pl.ds(pl.multiple_of(index * count, 8), count), cols)
            left[here] = left[here] + ref[...]

    for start in range(base, base + rows, SIZE):
        here = pl.ds(start, SIZE)
        left[:, here] = exact_t(left[:, here], ready_ref[here, here])
    if base:
        solved = pl.ds(0, base)
        left[:, part] = left[:, part] - exact_t(left[:, solved], ready_ref[part, solved])
    for start in range(base, base + rows, 2 * SIZE):
        first, second = pl.ds(start, SIZE), pl.ds(start + SIZE, SIZE)
        left[:, second] = left[:, second] - exact_t(left[:, first], ready_ref[second, first])
        below = pl.ds(start + 2 * SIZE, base + rows - start - 2 * SIZE)
        if below.size:
            both = pl.ds(start, 2 * SIZE)
            left[:, below] = left[:, below] - exact_t(left[:, both], ready_ref[below, both])


def solve_first_kernel(where_ref, ready_ref, right_own_ref, right_other_ref, kept_ref, arrived_ref, solved_ref):
    solve_part(0, where_ref, ready_ref, (right_own_ref, right_other_ref), kept_ref, arrived_ref, solved_ref)


def solve_second_kernel(
    where_ref, ready_ref, right_own_ref, right_other_ref, solved_ref, kept_ref, arrived_ref, *out_refs
):
    *piece_refs, left = out_refs
    strip = right_own_ref.shape[1]
    base = solved_ref.shape[1]
    left[:, pl.ds(0, base)] = solved_ref[...]
    solve_part(base, where_ref, ready_ref, (right_own_ref, right_other_ref), kept_ref, arrived_ref, left)
    for step, piece_ref in enumerate(piece_refs):
        piece_ref[...] = left[:, pl.ds(pl.multiple_of((where_ref[0] ^ step) * strip, strip), strip)]


def sum_kernel(where_ref, *refs):
    *piece_refs, own_ref, other_ref, total = refs
    value = piece_refs[0][...]
    for ref in piece_refs[1:]:
        value = value + ref[...]
    total[...] = value
    count = own_ref.shape[0]
    own_ref[...] = total[pl.ds(pl.multiple_of(where_ref[3] * count, 8), count), :]
    other_ref[...] = total[pl.ds(pl.multiple_of((1 - where_ref[3]) * count, 8), count), :]


def finish_kernel(cuts, where_ref, *refs):
    *part_refs, out_ref, total = refs
    offset = 0
    width = sum(cuts)
    for cut, own_ref, other_ref in zip(cuts, part_refs[::2], part_refs[1::2]):
        for ref, core in ((own_ref, where_ref[3]), (other_ref, 1 - where_ref[3])):
            for side in range(2):
                place = pl.multiple_of(side * 2 * width + core * width + offset, 8)
                total[pl.ds(place, cut), :] = ref[pl.ds(side * cut, cut), :]
        offset += cut
    out_ref[...] = total[...].T


def swap(value, axis, step):
    return lax.ppermute(value, axis, [(i, i ^ step) for i in range(lax.axis_size(axis))])


def shards(prev_solution, factor_panel, right_side, window_factor):
    row, group, side, core = (lax.axis_index(a) for a in ("row", "groups", "side", "core"))
    where = jnp.stack([row, group, side, core])
    strip_rows, strip_cols = right_side.shape
    window = window_factor.shape[1]
    width = prev_solution.shape[1]
    share_rows, half_window = strip_rows // 8, window // 2

    share = lax.dynamic_slice_in_dim(window_factor, (group * 4 + side * 2 + core) * share_rows, share_rows, 0)
    landed = [swap(share, "row", step) for step in (1, 2, 3)]
    right_own, right_other = call(
        right_kernel,
        [shape(2 * width, strip_rows)] * 2,
        [pltpu.VMEM((strip_cols, strip_rows), jnp.float32)],
        flops=5 * 10**10,
        scalars=1,
    )(where, right_side)
    panels = [factor_panel[:half_window], factor_panel[half_window:]]
    others = [swap(panel, "core", 1) for panel in panels]
    landed, right_own = lax.optimization_barrier((landed, right_own))
    right_other = swap(right_other, "core", 1)
    sizes = [shape(7, share_rows, strip_rows), shape(3, share_rows, strip_rows)]
    near, far = call(rows_kernel, sizes, scalars=1)(where, share, *landed)
    near, far = call(first_kernel, [shape(2, *size.shape) for size in sizes], scalars=1)(
        where, near, swap(near, "side", 1), far, swap(far, "groups", 1)
    )
    near, others, right_other = lax.optimization_barrier((near, others, right_other))
    shares = call(second_kernel, shape(4, 2, 2, share_rows, window), scalars=1)(
        where, near, swap(near, "groups", 1), far, swap(far, "side", 1)
    )

    dealt = call(deal_kernel, [shape(8, cut, 2 * factor_panel.shape[1]) for cut in QUERY_CUTS])(prev_solution.T)
    offset = 0
    parts = []
    for number, cut in enumerate(QUERY_CUTS):
        queries = lax.all_to_all(dealt[number], ("row", "side"), split_axis=0, concat_axis=0, tiled=True)
        queries = queries.reshape(8 * cut, -1)
        half = 4 * cut
        if not offset:
            queries, shares = lax.optimization_barrier((queries, shares))
        kept, far, high, low = call(
            couple_kernel,
            [shape(half, half_window)] * 2 + [shape(*queries.shape, dtype=jnp.bfloat16)] * 2,
            scalars=1,
        )(where, queries, panels[0], others[0])
        if not offset:
            far, shares = lax.optimization_barrier((far, shares))
            ready = call(
                prepare_kernel, shape(window, window), [pltpu.VMEM((window, window), jnp.float32)], scalars=1
            )(where, shares, swap(shares, "core", 1))
        kept_more, far_more = call(couple_more_kernel, [shape(half, half_window)] * 2)(high, low, panels[1], others[1])
        rights = (right_own, right_other)
        solved = call(solve_first_kernel, shape(half, half_window), scalars=1)(
            where, ready, *rights, kept, swap(far, "side", 1)
        )
        pieces = call(
            solve_second_kernel, [shape(half, strip_rows)] * 4, [pltpu.VMEM((half, window), jnp.float32)], scalars=1
        )(where, ready, *rights, solved, kept_more, swap(far_more, "side", 1))
        landed = [swap(pieces[step], "row", step) for step in (3, 2, 1)]
        own, other = call(
            sum_kernel, [shape(half // 2, strip_rows)] * 2, [pltpu.VMEM((half, strip_rows), jnp.float32)], scalars=1
        )(where, pieces[0], *landed)
        parts += [own, swap(other, "core", 1)]
        offset += cut
    return call(
        functools.partial(finish_kernel, QUERY_CUTS),
        shape(strip_rows, strip_cols),
        [pltpu.VMEM((strip_cols, strip_rows), jnp.float32)],
        scalars=1,
    )(where, *parts)


def shards_any(prev_solution, factor_panel, right_side, window_factor):
    row = lax.axis_index("row")
    strip_rows, strip_cols = right_side.shape
    by_rows = lax.all_to_all(prev_solution, ("row", "col"), split_axis=0, concat_axis=1, tiled=True)
    factor = lax.all_gather(window_factor, "row", axis=0, tiled=True)
    right = jnp.zeros((factor.shape[0], strip_cols), jnp.float32)
    right = lax.dynamic_update_slice_in_dim(right, right_side, row * strip_rows, 0)
    partial = exact(factor_panel, by_rows)
    coupling = lax.psum_scatter(partial, "col", scatter_dimension=1, tiled=True)
    solved = jax.scipy.linalg.solve_triangular(factor, right - coupling, lower=True)
    return lax.psum_scatter(solved, "row", scatter_dimension=0, tiled=True)


def solution(mesh):
    staged = mesh.shape["groups"] == 2 and mesh.shape["row"] == 4 and mesh.shape["col"] == 4
    if staged:
        mesh = Mesh(mesh.devices.reshape(2, 4, 2, 2), ("groups", "row", "side", "core"))
    col = ("side", "core") if staged else ("col",)
    in_specs = (P(None, ("groups", "row", *col)), P(None, ("row", *col)), P("row", ("groups", *col)), P("row", None))
    out_specs = P("row", ("groups", *col))
    body = shards if staged else shards_any
    return jax.shard_map(body, mesh=mesh, in_specs=in_specs, out_specs=out_specs, check_vma=False)
```

```python
import functools
import math

import jax
import jax.numpy as jnp
from jax import lax
from jax.experimental import pallas as pl
from jax.experimental.pallas import tpu as pltpu
from jax.sharding import Mesh
from jax.sharding import PartitionSpec as P

HIGHEST = lax.Precision.HIGHEST
SIZE = 128
VMEM = pl.BlockSpec(memory_space=pltpu.VMEM)
SMEM = pl.BlockSpec(memory_space=pltpu.SMEM)
TILE = 256
QUERY_CUTS = (32,)


def exact(a, b):
    return jnp.dot(a, b, precision=HIGHEST, preferred_element_type=jnp.float32)


def near(a, b):
    a_high, a_low = halves(a)
    b_high, b_low = halves(b)
    total = jnp.dot(a_high, b_low, preferred_element_type=jnp.float32)
    total = total + jnp.dot(a_low, b_high, preferred_element_type=jnp.float32)
    return total + jnp.dot(a_high, b_high, preferred_element_type=jnp.float32)


def exact_t(a, b):
    return lax.dot_general(a, b, (((1,), (1,)), ((), ())), precision=HIGHEST, preferred_element_type=jnp.float32)


def call(kernel, outs, scratch=(), flops=10**6, scalars=0, spare=4):
    def run(*args):
        moved = sum(a.size * a.dtype.itemsize for a in args)
        held = sum(math.prod(a.shape) * a.dtype.itemsize for a in (*jax.tree.leaves(outs), *scratch))
        return pl.pallas_call(
            kernel,
            out_shape=outs,
            in_specs=[SMEM] * scalars + [VMEM] * (len(args) - scalars),
            out_specs=jax.tree.map(lambda _: VMEM, outs),
            scratch_shapes=list(scratch),
            cost_estimate=pl.CostEstimate(flops=flops, bytes_accessed=moved, transcendentals=0),
            compiler_params=pltpu.CompilerParams(vmem_limit_bytes=moved + held + spare * 2**20),
        )(*args)

    return run


def shape(*dims, dtype=jnp.float32):
    return jax.ShapeDtypeStruct(dims, dtype)


def rows_kernel(where_ref, share_ref, *refs):
    *landed_refs, near_ref, far_ref = refs
    width = near_ref.shape[2]
    for step, ref in enumerate((share_ref, *landed_refs)):
        source = where_ref[0] ^ step
        near_ref[source] = ref[:, pl.ds(0, width)]
        for quarter, out_ref, first in ((1, near_ref, 3), (2, far_ref, -2), (3, far_ref, -1)):

            @pl.when(source >= quarter)
            def _(source=source, ref=ref, quarter=quarter, out_ref=out_ref, first=first):
                out_ref[source + first] = ref[:, pl.ds(quarter * width, width)]


def first_kernel(where_ref, near_ref, near_other_ref, far_ref, far_other_ref, near_out, far_out):
    row, group, side, core = (where_ref[i] for i in range(4))
    near_out[side] = near_ref[...]
    near_out[1 - side] = near_other_ref[...]
    far_out[group] = far_ref[...]
    far_out[1 - group] = far_other_ref[...]


def second_kernel(where_ref, near_ref, near_other_ref, far_ref, far_other_ref, out_ref):
    row, group, side, core = (where_ref[i] for i in range(4))
    width = near_ref.shape[3]
    zero = jnp.zeros(near_ref.shape[2:], jnp.float32)
    for r in range(4):
        for i in range(2):
            for quarter, first in enumerate((0, 3, -2, -1)):
                cols = pl.ds(quarter * width, width)
                if quarter < 2:
                    here, other = out_ref.at[r, group, i, :, cols], out_ref.at[r, 1 - group, i, :, cols]
                    refs = near_ref, near_other_ref
                else:
                    here, other = out_ref.at[r, i, side, :, cols], out_ref.at[r, i, 1 - side, :, cols]
                    refs = far_ref, far_other_ref
                here[...] = refs[0][i, r + first] if r >= quarter else zero
                other[...] = refs[1][i, r + first] if r >= quarter else zero


def prepare_kernel(where_ref, own_ref, other_ref, ready_ref, factor_ref):
    core = where_ref[3]
    count = own_ref.shape[3]
    for piece in range(16):
        at = (piece // 4, piece // 2 % 2, piece % 2)
        for ref, index in ((own_ref, core), (other_ref, 1 - core)):
            start = pl.multiple_of((2 * piece + index) * count, 8)
            factor_ref[pl.ds(start, count), :] = ref[at]
    rows = lax.broadcasted_iota(jnp.int32, (SIZE, SIZE), 0)
    cols = lax.broadcasted_iota(jnp.int32, (SIZE, SIZE), 1)
    starts = range(0, factor_ref.shape[0], SIZE)
    blocks = [factor_ref[pl.ds(s, SIZE), pl.ds(s, SIZE)] for s in starts]
    inverses = []
    below = (rows % 2 == 1) & (cols == rows - 1)
    for block in blocks:
        lane = 1.0 / jnp.sum(jnp.where(rows == cols, block, 0.0), axis=0, keepdims=True)
        sublane = 1.0 / jnp.sum(jnp.where(rows == cols, block, 0.0), axis=1, keepdims=True)
        inverses.append(jnp.where(rows == cols, sublane, 0.0) - jnp.where(below, sublane * block * lane, 0.0))
    step = 2
    while step < SIZE:
        below = ((rows // step) % 2 == 1) & (cols // step == rows // step - 1)
        coupled = [near(jnp.where(below, b, 0.0), i) for b, i in zip(blocks, inverses)]
        inverses = [i - near(i, c) for i, c in zip(inverses, coupled)]
        step *= 2
    lower = [jnp.where(rows >= cols, block, 0.0) for block in blocks]
    errors = [jnp.where(rows == cols, 1.0, 0.0) - exact(b, i) for b, i in zip(lower, inverses)]
    inverses = [i + near(i, e) for i, e in zip(inverses, errors)]
    for start, inverse in zip(starts, inverses):
        if start:
            ready_ref[pl.ds(start, SIZE), pl.ds(0, start)] = exact(
                inverse, factor_ref[pl.ds(start, SIZE), pl.ds(0, start)]
            )
        ready_ref[pl.ds(start, SIZE), pl.ds(start, SIZE)] = inverse


def right_kernel(where_ref, right_ref, own_ref, other_ref, by_query):
    core = where_ref[3]
    by_query[...] = right_ref[...].T
    width = own_ref.shape[0] // 2
    for side in range(2):
        for ref, index in ((own_ref, core), (other_ref, 1 - core)):
            start = pl.multiple_of((2 * side + index) * width, 8)
            ref[pl.ds(side * width, width), :] = by_query[pl.ds(start, width), :]


def halves(value):
    high = value.astype(jnp.bfloat16)
    return high, (value - high.astype(jnp.float32)).astype(jnp.bfloat16)


def split_kernel(where_ref, queries_ref, high_ref, low_ref):
    side, core = where_ref[2], where_ref[3]
    count, columns = queries_ref.shape[0] // 2, queries_ref.shape[1] // 2
    for part in range(2):
        rows = pl.ds(pl.multiple_of(((side + part) % 2) * count, 8), count)
        for half in range(2):
            cols = pl.ds(pl.multiple_of(((core + half) % 2) * columns, 128), columns)
            here = (pl.ds(part * count, count), pl.ds(half * columns, columns))
            high_ref[here], low_ref[here] = halves(queries_ref[rows, cols])


def multiply(high_ref, low_ref, panel_refs, kept_ref, far_ref):
    count, window = kept_ref.shape
    columns = panel_refs[0].shape[1]

    def product(a, b):
        return lax.dot_general(a, b, (((1,), (1,)), ((), ())), preferred_element_type=jnp.float32)

    for start in range(0, window, 256):
        here = pl.ds(start, 256)
        total = 0.0
        for half, ref in enumerate(panel_refs):
            cols = pl.ds(half * columns, columns)
            high, low = halves(ref[here, :])
            total = total + product(high_ref[:, cols], high)
            total = total + product(low_ref[:, cols], high) + product(high_ref[:, cols], low)
        kept_ref[:, here] = total[:count]
        far_ref[:, here] = total[count:]


def couple_kernel(where_ref, queries_ref, own_ref, other_ref, kept_ref, far_ref, high_ref, low_ref):
    @pl.when(pl.program_id(0) == 0)
    def _():
        split_kernel(where_ref, queries_ref, high_ref, low_ref)

    multiply(high_ref, low_ref, (own_ref, other_ref), kept_ref, far_ref)


def couple_more_kernel(high_ref, low_ref, own_ref, other_ref, kept_ref, far_ref):
    multiply(high_ref, low_ref, (own_ref, other_ref), kept_ref, far_ref)


def by_tiles(kernel, queries, panels, count, scalars=(), split=()):
    window, columns = panels[0].shape
    panel = pl.BlockSpec((TILE, columns), lambda i: (i, 0))
    out = pl.BlockSpec((count, TILE), lambda i: (0, i))
    return pl.pallas_call(
        kernel,
        grid=(window // TILE,),
        out_shape=[shape(count, window)] * 2 + list(split),
        in_specs=[SMEM] * len(scalars) + [VMEM] * len(queries) + [panel] * 2,
        out_specs=[out] * 2 + [pl.BlockSpec(s.shape, lambda i: (0, 0)) for s in split],
        cost_estimate=pl.CostEstimate(flops=10**6, bytes_accessed=10**7, transcendentals=0),
        compiler_params=pltpu.CompilerParams(vmem_limit_bytes=20 * 2**20),
    )(*scalars, *queries, *panels)


def deal_kernel(queries_ref, *out_refs):
    columns = out_refs[0].shape[2]
    offset = 0
    for out_ref in out_refs:
        for chip in range(8):
            out_ref[chip] = queries_ref[pl.ds(offset, out_ref.shape[1]), pl.ds(chip * columns, columns)]
        offset += out_ref.shape[1]


def solve_part(base, where_ref, ready_ref, right_refs, kept_ref, arrived_ref, left):
    count, strip = right_refs[0].shape
    rows = kept_ref.shape[1]
    row, core = where_ref[0], where_ref[3]
    part = pl.ds(base, rows)
    left[:, part] = -(kept_ref[...] + arrived_ref[...])

    @pl.when(row // (rows // strip) == base // rows)
    def _():
        cols = pl.ds(pl.multiple_of(row * strip, strip), strip)
        for ref, index in zip(right_refs, (core, 1 - core)):
            here = (pl.ds(pl.multiple_of(index * count, 8), count), cols)
            left[here] = left[here] + ref[...]

    for start in range(base, base + rows, SIZE):
        here = pl.ds(start, SIZE)
        left[:, here] = exact_t(left[:, here], ready_ref[here, here])
    if base:
        solved = pl.ds(0, base)
        left[:, part] = left[:, part] - exact_t(left[:, solved], ready_ref[part, solved])
    for start in range(base, base + rows, 2 * SIZE):
        first, second = pl.ds(start, SIZE), pl.ds(start + SIZE, SIZE)
        left[:, second] = left[:, second] - exact_t(left[:, first], ready_ref[second, first])
        below = pl.ds(start + 2 * SIZE, base + rows - start - 2 * SIZE)
        if below.size:
            both = pl.ds(start, 2 * SIZE)
            left[:, below] = left[:, below] - exact_t(left[:, both], ready_ref[below, both])


def solve_first_kernel(where_ref, ready_ref, right_own_ref, right_other_ref, kept_ref, arrived_ref, solved_ref):
    solve_part(0, where_ref, ready_ref, (right_own_ref, right_other_ref), kept_ref, arrived_ref, solved_ref)


def solve_second_kernel(
    where_ref, ready_ref, right_own_ref, right_other_ref, solved_ref, kept_ref, arrived_ref, *out_refs
):
    *piece_refs, left = out_refs
    strip = right_own_ref.shape[1]
    base = solved_ref.shape[1]
    left[:, pl.ds(0, base)] = solved_ref[...]
    solve_part(base, where_ref, ready_ref, (right_own_ref, right_other_ref), kept_ref, arrived_ref, left)
    for step, piece_ref in enumerate(piece_refs):
        piece_ref[...] = left[:, pl.ds(pl.multiple_of((where_ref[0] ^ step) * strip, strip), strip)]


def sum_kernel(where_ref, *refs):
    *piece_refs, own_ref, other_ref, total = refs
    value = piece_refs[0][...]
    for ref in piece_refs[1:]:
        value = value + ref[...]
    total[...] = value
    count = own_ref.shape[0]
    own_ref[...] = total[pl.ds(pl.multiple_of(where_ref[3] * count, 8), count), :]
    other_ref[...] = total[pl.ds(pl.multiple_of((1 - where_ref[3]) * count, 8), count), :]


def finish_kernel(cuts, where_ref, *refs):
    *part_refs, out_ref, total = refs
    offset = 0
    width = sum(cuts)
    for cut, own_ref, other_ref in zip(cuts, part_refs[::2], part_refs[1::2]):
        for ref, core in ((own_ref, where_ref[3]), (other_ref, 1 - where_ref[3])):
            for side in range(2):
                place = pl.multiple_of(side * 2 * width + core * width + offset, 8)
                total[pl.ds(place, cut), :] = ref[pl.ds(side * cut, cut), :]
        offset += cut
    out_ref[...] = total[...].T


def swap(value, axis, step):
    return lax.ppermute(value, axis, [(i, i ^ step) for i in range(lax.axis_size(axis))])


def shards(prev_solution, factor_panel, right_side, window_factor):
    row, group, side, core = (lax.axis_index(a) for a in ("row", "groups", "side", "core"))
    where = jnp.stack([row, group, side, core])
    strip_rows, strip_cols = right_side.shape
    window = window_factor.shape[1]
    width = prev_solution.shape[1]
    share_rows, half_window = strip_rows // 8, window // 2

    share = lax.dynamic_slice_in_dim(window_factor, (group * 4 + side * 2 + core) * share_rows, share_rows, 0)
    landed = [swap(share, "row", step) for step in (1, 2, 3)]
    right_own, right_other = call(
        right_kernel,
        [shape(2 * width, strip_rows)] * 2,
        [pltpu.VMEM((strip_cols, strip_rows), jnp.float32)],
        flops=5 * 10**10,
        scalars=1,
    )(where, right_side)
    panels = [factor_panel[:half_window], factor_panel[half_window:]]
    others = [swap(panel, "core", 1) for panel in panels]
    landed, right_own = lax.optimization_barrier((landed, right_own))
    right_other = swap(right_other, "core", 1)
    sizes = [shape(7, share_rows, strip_rows), shape(3, share_rows, strip_rows)]
    near, far = call(rows_kernel, sizes, scalars=1)(where, share, *landed)
    near, far = call(first_kernel, [shape(2, *size.shape) for size in sizes], scalars=1)(
        where, near, swap(near, "side", 1), far, swap(far, "groups", 1)
    )
    near, others, right_other = lax.optimization_barrier((near, others, right_other))
    shares = call(second_kernel, shape(4, 2, 2, share_rows, window), scalars=1)(
        where, near, swap(near, "groups", 1), far, swap(far, "side", 1)
    )

    dealt = call(deal_kernel, [shape(8, cut, 2 * factor_panel.shape[1]) for cut in QUERY_CUTS])(prev_solution.T)
    offset = 0
    parts = []
    for number, cut in enumerate(QUERY_CUTS):
        queries = lax.all_to_all(dealt[number], ("row", "side"), split_axis=0, concat_axis=0, tiled=True)
        queries = queries.reshape(8 * cut, -1)
        half = 4 * cut
        if not offset:
            queries, shares = lax.optimization_barrier((queries, shares))
        kept, far, high, low = by_tiles(
            couple_kernel,
            (queries,),
            (panels[0], others[0]),
            half,
            scalars=(where,),
            split=[shape(*queries.shape, dtype=jnp.bfloat16)] * 2,
        )
        if not offset:
            far, shares = lax.optimization_barrier((far, shares))
            ready = call(
                prepare_kernel, shape(window, window), [pltpu.VMEM((window, window), jnp.float32)], scalars=1
            )(where, shares, swap(shares, "core", 1))
        kept_more, far_more = by_tiles(couple_more_kernel, (high, low), (panels[1], others[1]), half)
        rights = (right_own, right_other)
        solved = call(solve_first_kernel, shape(half, half_window), scalars=1)(
            where, ready, *rights, kept, swap(far, "side", 1)
        )
        pieces = call(
            solve_second_kernel, [shape(half, strip_rows)] * 4, [pltpu.VMEM((half, window), jnp.float32)], scalars=1
        )(where, ready, *rights, solved, kept_more, swap(far_more, "side", 1))
        landed = [swap(pieces[step], "row", step) for step in (3, 2, 1)]
        own, other = call(
            sum_kernel, [shape(half // 2, strip_rows)] * 2, [pltpu.VMEM((half, strip_rows), jnp.float32)], scalars=1
        )(where, pieces[0], *landed)
        parts += [own, swap(other, "core", 1)]
        offset += cut
    return call(
        functools.partial(finish_kernel, QUERY_CUTS),
        shape(strip_rows, strip_cols),
        [pltpu.VMEM((strip_cols, strip_rows), jnp.float32)],
        scalars=1,
    )(where, *parts)


def shards_any(prev_solution, factor_panel, right_side, window_factor):
    row = lax.axis_index("row")
    strip_rows, strip_cols = right_side.shape
    by_rows = lax.all_to_all(prev_solution, ("row", "col"), split_axis=0, concat_axis=1, tiled=True)
    factor = lax.all_gather(window_factor, "row", axis=0, tiled=True)
    right = jnp.zeros((factor.shape[0], strip_cols), jnp.float32)
    right = lax.dynamic_update_slice_in_dim(right, right_side, row * strip_rows, 0)
    partial = exact(factor_panel, by_rows)
    coupling = lax.psum_scatter(partial, "col", scatter_dimension=1, tiled=True)
    solved = jax.scipy.linalg.solve_triangular(factor, right - coupling, lower=True)
    return lax.psum_scatter(solved, "row", scatter_dimension=0, tiled=True)


def solution(mesh):
    staged = mesh.shape["groups"] == 2 and mesh.shape["row"] == 4 and mesh.shape["col"] == 4
    if staged:
        mesh = Mesh(mesh.devices.reshape(2, 4, 2, 2), ("groups", "row", "side", "core"))
    col = ("side", "core") if staged else ("col",)
    in_specs = (P(None, ("groups", "row", *col)), P(None, ("row", *col)), P("row", ("groups", *col)), P("row", None))
    out_specs = P("row", ("groups", *col))
    body = shards if staged else shards_any
    return jax.shard_map(body, mesh=mesh, in_specs=in_specs, out_specs=out_specs, check_vma=False)
```
